32 devices in a mesh: pages: 2 (over y), tile: 8 (over z, x), mp: 2 (over core).
Axes of the slice: x: 2, y: 2, z: 4, core: 2. Of those that a mesh axis runs over, the one named last changes fastest.
Arguments:
- queries: bfloat16 [3072, 1024], P(('pages', 'tile'), 'mp'), parts along dimension 0, may hold values from -10.5 to 10.5
- key_rows: bfloat16 [3072, 1024], P(('pages', 'tile'), 'mp'), parts along dimension 0, may hold values from -8.5 to 8.5
- value_rows: bfloat16 [3072, 1024], P(('pages', 'tile'), 'mp'), parts along dimension 0, may hold values from -6 to 6
- grad_out: bfloat16 [3072, 1024], P(('pages', 'tile'), 'mp'), parts along dimension 0, may hold values from -6 to 6
- owner_shard: int32 [3072], P(('pages', 'tile')), parts along dimension 0, may hold values from 0 to 7, as said below
- logit_scale: float32 [16], P('mp'), may hold values from 0.5 to 2
Outputs:
- grad_queries: bfloat16 [3072, 1024], P(('pages', 'tile'), 'mp'), parts along dimension 0
- grad_keys: bfloat16 [3072, 1024], P(('pages', 'tile'), 'mp'), parts along dimension 0
- grad_values: bfloat16 [3072, 1024], P(('pages', 'tile'), 'mp'), parts along dimension 0
The draws below stay inside these ranges and needn't reach their ends.
There are 2 independent parts, one for each index of `pages`. The reference program is written for one: setup_inputs(seed, part) draws one part's arguments, and reference() takes and returns one part's arrays. A program takes and returns all parts, laid end to end along the dimension named above; an argument that names none is the same for every part. Nothing has to cross between parts.
Inputs may be any that keep to these rules, and one draw needn't show every extreme that they name: `owner_shard`: the 192 tokens of one index of tile name any one region at most 48 times; in every draw one region is named exactly 48 times by the tokens of every index of tile, so it holds 384 tokens.
All inputs are finite; a program needn't handle non-finite values.
Results may differ from the reference program's by a relative error of at most 0.0035.
The reference program's roundings to bfloat16 on the way count: a program that leaves them out, or rounds other values in their place, can miss the bound.
Values may be sent and summed in bfloat16 or wider, within the bound.
A program may use at most 64 MiB of HBM per device.

```python
import math
import jax
import jax.numpy as jnp
from jax import lax

H = 16
E = 64
TOK_DEV = 192
TOKENS = 1536
SHARDS = 8
SLOT = 48
CAPACITY = 384


def draw_queries(key, part):
    base = jnp.clip(jax.random.normal(jax.random.fold_in(key, 32), (TOKENS, H * E), jnp.float32), -4.5, 4.5)
    return base.astype(jnp.bfloat16)


def draw_key_rows(key, part):
    base = jnp.clip(jax.random.normal(jax.random.fold_in(key, 34), (TOKENS, H * E), jnp.float32), -4.5, 4.5)
    return base.astype(jnp.bfloat16)


def draw_owner_shard(key, part):
    favored = jax.random.randint(jax.random.fold_in(key, 21), (), 0, SHARDS)
    pull_level = jax.random.randint(jax.random.fold_in(key, 22), (SHARDS,), 0, 3)
    noise_bits = jax.random.randint(jax.random.fold_in(key, 23), (SHARDS, SHARDS, SLOT), 0, 512)
    dest_ids = jnp.arange(SHARDS, dtype=jnp.int32)
    priority = noise_bits + 256 * pull_level[None, :, None] + 4096 * (dest_ids == favored).astype(jnp.int32)[None, :, None]
    flat_priority = priority.reshape(SHARDS, SHARDS * SLOT) * (SHARDS * SLOT) + jnp.arange(SHARDS * SLOT, dtype=jnp.int32)[None, :]
    chosen = lax.top_k(flat_priority, TOK_DEV)[1]
    dest_shard = (chosen // SLOT).astype(jnp.int32)
    order_keys = jax.random.randint(jax.random.fold_in(key, 24), (SHARDS, TOK_DEV), 0, 1 << 20) * TOK_DEV + jnp.arange(TOK_DEV, dtype=jnp.int32)[None, :]
    shuffle = jnp.argsort(order_keys, axis=1)
    mixed = jnp.take_along_axis(dest_shard, shuffle, axis=1)
    return mixed.reshape(TOKENS).astype(jnp.int32)


def block_scale(own_key, dims, shards, smallest, largest):
    gain, own = 1.0, jax.random.fold_in(own_key, 6)
    for dim, blocks in shards:
        steps = jnp.exp(jax.random.uniform(jax.random.fold_in(own, dim), (blocks,), jnp.float32, smallest / len(shards), largest / len(shards)))
        gain = gain * jnp.repeat(steps, dims[dim] // blocks).reshape([-1 if axis == dim else 1 for axis in range(len(dims))])
    return gain


def noise(key, shape, scale, most, pieces=(), held_as=jnp.bfloat16):
    entries = jax.random.normal(key, shape, jnp.float32) * scale
    if len(pieces) > 0:
        entries = block_scale(key, shape, pieces, -0.22, 0.18) * entries
    return jnp.clip(entries, min=-most, max=most).astype(held_as)


def setup_inputs(seed: int = 0, part: int = 0) -> dict:
    keys = jax.random.split(jax.random.key(seed), 7)
    own_keys = jax.random.split(jax.random.fold_in(keys[6], part), 7)
    queries = draw_queries(jax.random.fold_in(jax.random.fold_in(keys[6], part), 71), part)
    key_rows = draw_key_rows(jax.random.fold_in(jax.random.fold_in(keys[6], part), 71), part)
    value_rows = noise(own_keys[2], (TOKENS, H * E), 1.0, 6.0, ((0, 8), (1, 2)))
    grad_out = noise(own_keys[3], (TOKENS, H * E), 1.0, 6.0, ((0, 8), (1, 2)))
    owner_shard = draw_owner_shard(jax.random.fold_in(jax.random.fold_in(keys[6], part), 71), part)
    logit_scale = jnp.clip(jnp.exp(math.log(2.0) - 1.3862944 * jax.random.uniform(keys[5], (H,), jnp.float32) ** block_scale(keys[5], (H,), ((0, 2),), -0.2, 0.2)), 0.5, 2.0)
    return dict(queries=queries, key_rows=key_rows, value_rows=value_rows, grad_out=grad_out, owner_shard=owner_shard, logit_scale=logit_scale)


def attend_heads(query_heads, key_heads, value_heads, dout_heads, live_rows):
    pair_mask = live_rows[None, :, None] & live_rows[None, None, :]
    scores = jnp.einsum('ihe,jhe->hij', query_heads, key_heads, preferred_element_type=jnp.float32)
    scores = jnp.where(pair_mask, scores, -1e+30)
    row_max = lax.optimization_barrier(jnp.max(scores, axis=2, keepdims=True))
    raw_weights = jnp.where(pair_mask, jnp.exp(scores - row_max), 0.0)
    row_sum = lax.optimization_barrier(jnp.sum(raw_weights, axis=2, keepdims=True))
    row_sum = jnp.where(live_rows[None, :, None], row_sum, 1.0)
    weights = raw_weights / row_sum
    weights_low = weights.astype(jnp.bfloat16)
    attended = jnp.einsum('hij,jhe->ihe', weights_low, value_heads, preferred_element_type=jnp.float32)
    row_delta = lax.optimization_barrier(jnp.sum(dout_heads.astype(jnp.float32) * attended, axis=2))
    dprobs = jnp.einsum('ihe,jhe->hij', dout_heads, value_heads, preferred_element_type=jnp.float32)
    dscores = (weights * (dprobs - jnp.transpose(row_delta)[:, :, None])).astype(jnp.bfloat16)
    grad_value = jnp.einsum('hij,ihe->jhe', weights_low, dout_heads, preferred_element_type=jnp.float32).astype(jnp.bfloat16)
    grad_key = jnp.einsum('hij,ihe->jhe', dscores, query_heads, preferred_element_type=jnp.float32).astype(jnp.bfloat16)
    grad_raw = jnp.einsum('hij,jhe->ihe', dscores, key_heads, preferred_element_type=jnp.float32).astype(jnp.bfloat16)
    return (grad_raw, grad_key, grad_value)

def reference(queries, key_rows, value_rows, grad_out, owner_shard, logit_scale):
    scale_cols = jnp.repeat(logit_scale / math.sqrt(E), E)
    scaled = (queries.astype(jnp.float32) * scale_cols).astype(jnp.bfloat16)

    def region_step(carry, shard):
        found = jnp.nonzero(owner_shard == shard, size=CAPACITY, fill_value=TOKENS)[0].astype(jnp.int32)
        live_rows = found < TOKENS
        safe_rows = jnp.minimum(found, TOKENS - 1)

        def pick_rows(source):
            return source[safe_rows].reshape(CAPACITY, H, E)
        results = attend_heads(pick_rows(scaled), pick_rows(key_rows), pick_rows(value_rows), pick_rows(grad_out), live_rows)
        target = jnp.where(live_rows, found, TOKENS)
        updated = tuple((held.at[target].set(piece.reshape(CAPACITY, H * E).astype(held.dtype), mode='drop') for held, piece in zip(carry, results)))
        return (updated, None)
    blank = jnp.zeros((TOKENS, H * E), jnp.bfloat16)
    final, _ = lax.scan(region_step, (blank, blank, blank), jnp.arange(SHARDS, dtype=jnp.int32))
    grad_queries = (final[0].astype(jnp.float32) * scale_cols).astype(jnp.bfloat16)
    return (grad_queries, final[1], final[2])
```

```python
import functools
import math

import jax
import jax.numpy as jnp
from jax import lax
from jax.experimental import pallas as pl
from jax.experimental.pallas import tpu as pltpu
from jax.sharding import PartitionSpec as P

MESH = pl.DeviceIdType.MESH
CONTRACT_LANES = (((1,), (1,)), ((), ()))


def dot(left, right):
    return jnp.dot(left, right, preferred_element_type=jnp.float32)


def swap_halves(tile):
    return pltpu.roll(tile, tile.shape[1] // 2, 1)


def exchange_kernel(
    n,
    slot,
    head_size,
    ids_hbm,
    scale_hbm,
    q_hbm,
    k_hbm,
    v_hbm,
    g_hbm,
    back_kq,
    back_v,
    ids_ref,
    scale_ref,
    q_ref,
    k_ref,
    v_ref,
    g_ref,
    send_place,
    send_qk,
    send_g,
    send_v,
    got_place,
    got_qk,
    got_g,
    got_v,
    region_qk,
    region_k,
    region_kt,
    region_g,
    region_v,
    bias,
    probs,
    probs_low,
    dscores,
    out_v,
    out_kq,
    ret_v,
    ret_kq,
    load_sem,
    send_sem,
    recv_sem,
):
    me = lax.axis_index("tile")
    tokens = q_ref.shape[0]
    capacity = n * slot
    width = 2 * head_size
    half = tokens // 2
    f32, bf16 = jnp.float32, jnp.bfloat16
    root = 1.0 / math.sqrt(head_size)

    barrier = pltpu.get_barrier_semaphore()
    for d in range(1, n):
        pl.semaphore_signal(
            barrier, inc=1, device_id={"tile": lax.rem(me + d, n)}, device_id_type=MESH
        )
    loads = [
        pltpu.make_async_copy(src, dst, load_sem.at[i])
        for i, (src, dst) in enumerate(
            (
                (q_hbm, q_ref),
                (k_hbm, k_ref),
                (g_hbm, g_ref),
                (v_hbm, v_ref),
                (ids_hbm, ids_ref),
                (scale_hbm, scale_ref),
            )
        )
    ]
    for i in (4, 5, 0, 1, 2, 3):
        loads[i].start()

    def low_lanes(rows):
        return lax.broadcasted_iota(jnp.int32, (rows, width), 1) < head_size

    loads[4].wait()
    ids = ids_ref[...]
    mine = (lax.broadcasted_iota(jnp.int32, (n, tokens), 0) == ids).astype(f32)
    earlier = (
        lax.broadcasted_iota(jnp.int32, (tokens, tokens), 0)
        < lax.broadcasted_iota(jnp.int32, (tokens, tokens), 1)
    ).astype(bf16)
    rank = jnp.sum(dot(mine.astype(bf16), earlier) * mine, axis=0, keepdims=True)
    send_place[...] = ids.astype(f32) * slot + rank

    low, low_half, low_cap = low_lanes(tokens), low_lanes(half), low_lanes(capacity)
    pairs = [
        (2 * pair, 2 * pair + 1, slice(pair * width, (pair + 1) * width))
        for pair in range(n // 2)
    ]
    loads[5].wait()
    loads[0].wait()
    loads[1].wait()
    for one, two, cols in pairs:
        lane_scale = jnp.where(low, scale_ref[one] * root, scale_ref[two] * root)
        q = (q_ref[:, cols].astype(f32) * lane_scale).astype(bf16).astype(f32)
        k = k_ref[:, cols].astype(f32)
        send_qk[one] = jnp.where(low, q, swap_halves(k)).astype(bf16)
        send_qk[two] = jnp.where(low, swap_halves(q), k).astype(bf16)

    pl.semaphore_wait(barrier, n - 1)

    def remote(kind, d, src, dst, peer):
        copy = pltpu.make_async_remote_copy(
            src_ref=src,
            dst_ref=dst,
            send_sem=send_sem.at[kind, d],
            recv_sem=recv_sem.at[kind, d],
            device_id={"tile": peer},
            device_id_type=MESH,
        )
        copy.start()
        return copy

    order = sorted(range(1, n), key=lambda d: -min(d, n - d))
    place_copies, qk_copies, g_copies, v_copies = {}, {}, {}, {}
    for d in order:
        place_copies[d] = remote(0, d, send_place, got_place.at[d], lax.rem(me + d, n))
    for d in order:
        peer = lax.rem(me + d, n)
        qk_copies[d] = remote(1, d, send_qk.at[peer], got_qk.at[d], peer)

    def fold(ref, send, load):
        load.wait()
        for one, two, cols in pairs:
            top, bottom = ref[:half, cols].astype(f32), ref[half:, cols].astype(f32)
            send[one] = jnp.where(low_half, top, swap_halves(bottom)).astype(bf16)
            send[two] = jnp.where(low_half, swap_halves(top), bottom).astype(bf16)

    fold(g_ref, send_g, loads[2])
    for d in order:
        peer = lax.rem(me + d, n)
        g_copies[d] = remote(2, d, send_g.at[peer], got_g.at[d], peer)
    fold(v_ref, send_v, loads[3])
    for d in order:
        peer = lax.rem(me + d, n)
        v_copies[d] = remote(3, d, send_v.at[peer], got_v.at[d], peer)

    got_place[0] = send_place[...]
    for d in order:
        place_copies[d].wait_recv()

    counts = jnp.zeros((n, capacity), f32)
    table = jnp.zeros((8, tokens), f32)
    slot_of = lax.broadcasted_iota(jnp.int32, (n, capacity), 1)
    region_row = lax.broadcasted_iota(jnp.int32, (n, tokens), 0).astype(f32) * slot
    for d in range(n):
        place = jnp.broadcast_to(got_place[d], (8, tokens))
        held = (place >= region_row) & (place < region_row + slot)
        count = jnp.sum(held.astype(f32), axis=1, keepdims=True)
        here = (slot_of >= d * slot) & (slot_of < (d + 1) * slot)
        counts = jnp.where(here, count + d * slot, counts)
        table = jnp.where(lax.broadcasted_iota(jnp.int32, (8, tokens), 0) == d, place, table)
    bias_cols = jnp.transpose(jnp.where(slot_of.astype(f32) < counts, 0.0, -1e30))
    for r in range(n):
        bias[r] = jnp.broadcast_to(bias_cols[:, r : r + 1], (capacity, 128))
    place_cols = jnp.transpose(table)

    def pick(d):
        rows = lax.broadcasted_iota(jnp.int32, (capacity, tokens), 0).astype(f32)
        return (rows == got_place[d]).astype(bf16)

    for d in order:
        qk_copies[d].wait_recv()
    for d in range(n):
        block = got_qk[d] if d else send_qk[me]
        placed = dot(pick(d), block)
        key_low = jnp.where(low_cap, swap_halves(placed), 0.0)
        region_qk[:, d] = placed.astype(bf16).reshape(n, slot, width)
        region_k[:, d] = key_low.astype(bf16).reshape(n, slot, width)

    blocks = [slice(b * 128, (b + 1) * 128) for b in range(capacity // 128)]

    def score_step(r, carry):
        qk = region_qk[r].reshape(capacity, width)
        key_low = region_k[r].reshape(capacity, width)
        for b in blocks:
            scores = lax.dot_general(
                key_low, qk[b], CONTRACT_LANES, preferred_element_type=f32
            ) + bias[r]
            raw = jnp.exp(scores - jnp.max(scores, axis=0, keepdims=True))
            weights = raw * (1.0 / jnp.sum(raw, axis=0, keepdims=True))
            probs[r, :, b] = weights
            probs_low[r, :, b] = weights.astype(bf16)
        region_kt[r] = jnp.transpose(qk.astype(f32))[head_size:].astype(bf16)
        return carry

    lax.fori_loop(0, n, score_step, 0, unroll=n)

    def unfold(got, send, d):
        folded = (got[d] if d else send[me]).astype(f32)
        return jnp.concatenate([folded, swap_halves(folded)], axis=0).astype(bf16)

    for d in order:
        g_copies[d].wait_recv()
    for d in range(n):
        placed = dot(pick(d), unfold(got_g, send_g, d))
        region_g[:, d] = placed.astype(bf16).reshape(n, slot, width)

    def value_step(r, carry):
        grads = dot(probs_low[r], region_g[r].reshape(capacity, width))
        out_v[:, r] = grads.astype(bf16).reshape(n, slot, width)
        return carry

    lax.fori_loop(0, n, value_step, 0, unroll=n)

    def put(d, source):
        lanes = lax.broadcasted_iota(jnp.int32, (tokens, capacity), 1).astype(f32)
        rows = (lanes == place_cols[:, d : d + 1]).astype(bf16)
        return dot(rows, source[d].reshape(capacity, width))

    batches = (order[: n // 2], order[n // 2 :] + [0])
    back_copies = []
    for batch in batches:
        for d in batch:
            grads = put(d, out_v)
            grads = jnp.where(low_half, grads[:half], swap_halves(grads[half:])).astype(bf16)
            if d:
                ret_v[d] = grads
            else:
                back_v[me] = grads
        for d in batch:
            if d:
                peer = lax.rem(me + n - d, n)
                back_copies.append(remote(4, d, ret_v.at[d], back_v.at[me], peer))

    for d in order:
        v_copies[d].wait_recv()
    for d in range(n):
        placed = jnp.where(low_cap, dot(pick(d), unfold(got_v, send_v, d)), 0.0)
        region_v[:, d] = placed.astype(bf16).reshape(n, slot, width)

    my_scale = scale_ref[me] * root

    def grad_step(r, carry):
        value_low = region_v[r].reshape(capacity, width)
        g = region_g[r].reshape(capacity, width)
        for b in blocks:
            dprobs = lax.dot_general(
                value_low, g[b], CONTRACT_LANES, preferred_element_type=f32
            )
            delta = jnp.sum(
                probs_low[r, :, b].astype(f32) * dprobs, axis=0, keepdims=True
            )
            dscores[r, :, b] = (probs[r, :, b] * (dprobs - delta)).astype(bf16)
        grads = dot(dscores[r], region_qk[r].reshape(capacity, width))
        raw_t = dot(region_kt[r], dscores[r]).astype(bf16).astype(f32) * my_scale
        raw = jnp.transpose(jnp.concatenate([raw_t, raw_t], axis=0))
        grads = jnp.where(low_cap, grads, raw)
        out_kq[:, r] = grads.astype(bf16).reshape(n, slot, width)
        return carry

    lax.fori_loop(0, n, grad_step, 0, unroll=n)

    for batch in batches:
        for d in batch:
            grads = put(d, out_kq).astype(bf16)
            if d:
                ret_kq[d] = grads
            else:
                back_kq[me] = grads
        for d in batch:
            if d:
                peer = lax.rem(me + n - d, n)
                back_copies.append(remote(5, d, ret_kq.at[d], back_kq.at[me], peer))
    for copy in back_copies:
        copy.wait_recv()
    for copies in (place_copies, qk_copies, g_copies, v_copies):
        for copy in copies.values():
            copy.wait_send()
    for copy in back_copies:
        copy.wait_send()


def unpack_kernel(n, kq_ref, v_ref, oq_ref, ok_ref, ov_ref):
    tokens, width = kq_ref.shape[1:]
    half = tokens // 2
    f32, bf16 = jnp.float32, jnp.bfloat16
    low = lax.broadcasted_iota(jnp.int32, (tokens, width), 1) < width // 2
    low_half = lax.broadcasted_iota(jnp.int32, (half, width), 1) < width // 2
    for pair in range(n // 2):
        cols = slice(pair * width, (pair + 1) * width)
        kq0, kq1 = kq_ref[2 * pair].astype(f32), kq_ref[2 * pair + 1].astype(f32)
        v0, v1 = v_ref[2 * pair].astype(f32), v_ref[2 * pair + 1].astype(f32)
        ok_ref[:, cols] = jnp.where(low, kq0, swap_halves(kq1)).astype(bf16)
        oq_ref[:, cols] = jnp.where(low, swap_halves(kq0), kq1).astype(bf16)
        ov_ref[:half, cols] = jnp.where(low_half, v0, swap_halves(v1)).astype(bf16)
        ov_ref[half:, cols] = jnp.where(low_half, swap_halves(v0), v1).astype(bf16)


def by_heads(queries, key_rows, value_rows, grad_out, owner_shard, logit_scale):
    n = lax.axis_size("tile")
    tokens, columns = queries.shape
    head_size = columns // n
    capacity = 2 * tokens
    slot = capacity // n
    width = 2 * head_size
    bf16, f32 = jnp.bfloat16, jnp.float32
    vmem = pl.BlockSpec(memory_space=pltpu.VMEM)
    anywhere = pl.BlockSpec(memory_space=pltpu.HBM)
    full = pltpu.VMEM((n, tokens, width), bf16)
    folded = pltpu.VMEM((n, tokens // 2, width), bf16)
    region = pltpu.VMEM((n, n, slot, width), bf16)
    square = (n, capacity, capacity)
    grant = 67043328 - 3 * n * tokens * width - 64 * 1024
    back_kq, back_v = pl.pallas_call(
        functools.partial(exchange_kernel, n, slot, head_size),
        out_shape=(
            pltpu.VMEM((n, tokens, width), bf16),
            pltpu.VMEM((n, tokens // 2, width), bf16),
        ),
        in_specs=[anywhere] * 6,
        out_specs=(vmem, vmem),
        scratch_shapes=[pltpu.VMEM((1, tokens), jnp.int32), pltpu.SMEM((n,), f32)]
        + [pltpu.VMEM((tokens, columns), bf16)] * 4
        + [pltpu.VMEM((1, tokens), f32), full, folded, folded]
        + [pltpu.VMEM((n, 1, tokens), f32), full, folded, folded]
        + [region, region, pltpu.VMEM((n, head_size, capacity), bf16), region, region]
        + [pltpu.VMEM((n, capacity, 128), f32), pltpu.VMEM(square, f32)]
        + [pltpu.VMEM(square, bf16), pltpu.VMEM(square, bf16)]
        + [region, region, folded, full]
        + [pltpu.SemaphoreType.DMA((6,))]
        + [pltpu.SemaphoreType.DMA((6, n))] * 2,
        compiler_params=pltpu.CompilerParams(
            collective_id=0, has_side_effects=True, vmem_limit_bytes=grant
        ),
    )(owner_shard.reshape(1, tokens), logit_scale, queries, key_rows, value_rows, grad_out)
    out = jax.ShapeDtypeStruct((tokens, columns), bf16)
    return pl.pallas_call(
        functools.partial(unpack_kernel, n),
        out_shape=(out, out, out),
        in_specs=[vmem, vmem],
        out_specs=(vmem, vmem, vmem),
        compiler_params=pltpu.CompilerParams(vmem_limit_bytes=8 * 1024 * 1024),
    )(back_kq, back_v)


def attend_heads(query_heads, key_heads, value_heads, dout_heads, live_rows):
    pair_mask = live_rows[None, :, None] & live_rows[None, None, :]
    scores = jnp.einsum("ihe,jhe->hij", query_heads, key_heads, preferred_element_type=jnp.float32)
    scores = jnp.where(pair_mask, scores, -1e30)
    row_max = jnp.max(scores, axis=2, keepdims=True)
    raw_weights = jnp.where(pair_mask, jnp.exp(scores - row_max), 0.0)
    row_sum = jnp.sum(raw_weights, axis=2, keepdims=True)
    row_sum = jnp.where(live_rows[None, :, None], row_sum, 1.0)
    weights = raw_weights / row_sum
    weights_low = weights.astype(jnp.bfloat16)
    attended = jnp.einsum(
        "hij,jhe->ihe", weights_low, value_heads, preferred_element_type=jnp.float32
    )
    row_delta = jnp.sum(dout_heads.astype(jnp.float32) * attended, axis=2)
    dprobs = jnp.einsum("ihe,jhe->hij", dout_heads, value_heads, preferred_element_type=jnp.float32)
    dscores = (weights * (dprobs - jnp.transpose(row_delta)[:, :, None])).astype(jnp.bfloat16)
    grad_value = jnp.einsum(
        "hij,ihe->jhe", weights_low, dout_heads, preferred_element_type=jnp.float32
    ).astype(jnp.bfloat16)
    grad_key = jnp.einsum(
        "hij,ihe->jhe", dscores, query_heads, preferred_element_type=jnp.float32
    ).astype(jnp.bfloat16)
    grad_raw = jnp.einsum(
        "hij,jhe->ihe", dscores, key_heads, preferred_element_type=jnp.float32
    ).astype(jnp.bfloat16)
    return (grad_raw, grad_key, grad_value)


def attend_items(query_items, key_items, value_items, dout_items, live_rows):
    capacity = query_items.shape[0]
    item_count = query_items.shape[1]
    head_size = query_items.shape[2] // 2
    outputs = ([], [], [])
    for item_index in range(item_count):
        halves = ([], [], [])
        for half_index in range(2):
            lower = half_index * head_size
            upper = lower + head_size
            pieces = attend_heads(
                query_items[:, item_index, lower:upper].reshape(capacity, 1, head_size),
                key_items[:, item_index, lower:upper].reshape(capacity, 1, head_size),
                value_items[:, item_index, lower:upper].reshape(capacity, 1, head_size),
                dout_items[:, item_index, lower:upper].reshape(capacity, 1, head_size),
                live_rows,
            )
            for holder, piece in zip(halves, pieces):
                holder.append(piece.reshape(capacity, head_size))
        for holder, parts_list in zip(outputs, halves):
            holder.append(jnp.concatenate(parts_list, axis=1))
    return tuple((jnp.stack(holder, axis=1) for holder in outputs))


def slot_places(owner_shard, shards, slot):
    one_hot = (owner_shard[:, None] == jnp.arange(shards, dtype=jnp.int32)[None, :]).astype(
        jnp.int32
    )
    before = jnp.cumsum(one_hot, axis=0) - one_hot
    rank = jnp.sum(before * one_hot, axis=1)
    return owner_shard * slot + rank


def by_regions(queries, key_rows, value_rows, grad_out, owner_shard, logit_scale):
    shards = lax.axis_size("tile")
    tok_rows, columns = queries.shape
    heads_here = logit_scale.shape[0]
    head_size = columns // heads_here
    capacity = 2 * tok_rows
    slot = capacity // shards
    pairs = heads_here // 2
    width = 2 * head_size
    slot_index = slot_places(owner_shard, shards, slot)
    scale_cols = jnp.repeat(logit_scale / math.sqrt(head_size), head_size)
    scaled = (queries.astype(jnp.float32) * scale_cols).astype(jnp.bfloat16)

    def spread(source):
        return jnp.zeros((capacity,) + source.shape[1:], source.dtype).at[slot_index].set(source)

    sent_query = spread(scaled)
    sent_key = spread(key_rows)
    sent_value = spread(value_rows)
    sent_dout = spread(grad_out)
    flags = spread(jnp.ones((tok_rows,), jnp.int32))
    got_query, got_key, got_value, got_dout, got_flags = (
        lax.all_to_all(sent_query, "tile", split_axis=0, concat_axis=0, tiled=True),
        lax.all_to_all(sent_key, "tile", split_axis=0, concat_axis=0, tiled=True),
        lax.all_to_all(sent_value, "tile", split_axis=0, concat_axis=0, tiled=True),
        lax.all_to_all(sent_dout, "tile", split_axis=0, concat_axis=0, tiled=True),
        lax.all_to_all(flags, "tile", split_axis=0, concat_axis=0, tiled=True),
    )
    grad_raw, grad_key, grad_value = attend_items(
        got_query.reshape(capacity, pairs, width),
        got_key.reshape(capacity, pairs, width),
        got_value.reshape(capacity, pairs, width),
        got_dout.reshape(capacity, pairs, width),
        got_flags > 0,
    )
    returned = (
        lax.all_to_all(
            grad_raw.reshape(capacity, columns), "tile", split_axis=0, concat_axis=0, tiled=True
        ),
        lax.all_to_all(
            grad_key.reshape(capacity, columns), "tile", split_axis=0, concat_axis=0, tiled=True
        ),
        lax.all_to_all(
            grad_value.reshape(capacity, columns), "tile", split_axis=0, concat_axis=0, tiled=True
        ),
    )
    grad_queries = (returned[0][slot_index].astype(jnp.float32) * scale_cols).astype(jnp.bfloat16)
    return (grad_queries, returned[1][slot_index], returned[2][slot_index])


def local(queries, key_rows, value_rows, grad_out, owner_shard, logit_scale):
    shards = lax.axis_size("tile")
    tokens, columns = queries.shape
    heads_here = logit_scale.shape[0]
    slot = 2 * tokens // shards
    fits = (
        shards == heads_here == 8
        and columns == heads_here * 64
        and slot % 16 == 0
        and (2 * tokens) % 128 == 0
        and tokens % 32 == 0
    )
    plan = by_heads if fits else by_regions
    return plan(queries, key_rows, value_rows, grad_out, owner_shard, logit_scale)


def solution(mesh):
    return jax.shard_map(
        local,
        mesh=mesh,
        in_specs=(
            P(("pages", "tile"), "mp"),
            P(("pages", "tile"), "mp"),
            P(("pages", "tile"), "mp"),
            P(("pages", "tile"), "mp"),
            P(("pages", "tile")),
            P("mp"),
        ),
        out_specs=(
            P(("pages", "tile"), "mp"),
            P(("pages", "tile"), "mp"),
            P(("pages", "tile"), "mp"),
        ),
        check_vma=False,
    )
```

```python
import functools
import math

import jax
import jax.numpy as jnp
from jax import lax
from jax.experimental import pallas as pl
from jax.experimental.pallas import tpu as pltpu
from jax.sharding import PartitionSpec as P

MESH = pl.DeviceIdType.MESH
CONTRACT_LANES = (((1,), (1,)), ((), ()))


def dot(left, right):
    return jnp.dot(left, right, preferred_element_type=jnp.float32)


def swap_halves(tile):
    return pltpu.roll(tile, tile.shape[1] // 2, 1)


def exchange_kernel(
    n,
    slot,
    head_size,
    ids_hbm,
    scale_hbm,
    q_hbm,
    k_hbm,
    v_hbm,
    g_hbm,
    back_kq,
    back_v,
    ids_ref,
    scale_ref,
    rows_ref,
    send_place,
    send_qk,
    send_g,
    send_v,
    got_place,
    got_qk,
    got_g,
    got_v,
    region_q,
    region_qk,
    region_k,
    region_g,
    region_v,
    bias,
    probs,
    probs_low,
    dscores,
    out_v,
    out_kq,
    ret_v,
    ret_kq,
    load_sem,
    send_sem,
    recv_sem,
):
    me = lax.axis_index("tile")
    tokens = send_place.shape[1]
    capacity = n * slot
    width = 2 * head_size
    half = tokens // 2
    f32, bf16 = jnp.float32, jnp.bfloat16
    root = 1.0 / math.sqrt(head_size)

    barrier = pltpu.get_barrier_semaphore()
    for d in range(1, n):
        pl.semaphore_signal(
            barrier, inc=1, device_id={"tile": lax.rem(me + d, n)}, device_id_type=MESH
        )
    loads = [
        pltpu.make_async_copy(src, dst, load_sem.at[i])
        for i, (src, dst) in enumerate(
            (
                (ids_hbm, ids_ref),
                (q_hbm, rows_ref.at[0]),
                (k_hbm, rows_ref.at[1]),
                (scale_hbm, scale_ref),
                (g_hbm, rows_ref.at[2]),
                (v_hbm, rows_ref.at[3]),
            )
        )
    ]
    for load in loads:
        load.start()

    def wait_bytes(refs, sem):
        pltpu.make_async_copy(refs, refs, sem).wait()

    bits = [me % 2, me // 2 % 2, me // 4]

    def across(d):
        flips = [d % 2, d // 2 % 2, d // 4]
        return sum((1 - b if f else b) * 2**i for i, (b, f) in enumerate(zip(bits, flips)))

    inner = (bits[1] + bits[2]) % 2
    early, late = (4, 5), (6, 7, 2, 3, 1)
    steps = list(zip((4, 5, 6, 7, 2, 3, 1), (2, 3, 1, 4, 5, 6, 7)))

    def pick_step(outside, inside):
        return outside + inner * (inside - outside)

    def remote(src, dst, send, recv, peer):
        pltpu.make_async_remote_copy(
            src_ref=src,
            dst_ref=dst,
            send_sem=send_sem.at[send],
            recv_sem=recv_sem.at[recv],
            device_id={"tile": peer},
            device_id_type=MESH,
        ).start()

    def scatter(send, got, kind, groups):
        for a, b in steps:
            d = pick_step(a, b)
            peer = pick_step(across(a), across(b))
            group = pick_step(groups[a in early], groups[b in early])
            remote(send.at[peer], got.at[d], kind, group, peer)

    def low_lanes(rows):
        return lax.broadcasted_iota(jnp.int32, (rows, width), 1) < head_size

    low, low_half, low_cap = low_lanes(tokens), low_lanes(half), low_lanes(capacity)
    pairs = [
        (2 * pair, 2 * pair + 1, slice(pair * width, (pair + 1) * width))
        for pair in range(n // 2)
    ]
    for load in loads[:4]:
        load.wait()
    for one, two, cols in pairs:
        lane_scale = jnp.where(low, scale_ref[one] * root, scale_ref[two] * root)
        q = (rows_ref[0, :, cols].astype(f32) * lane_scale).astype(bf16).astype(f32)
        k = rows_ref[1, :, cols].astype(f32)
        send_qk[one] = jnp.where(low, q, swap_halves(k)).astype(bf16)
        send_qk[two] = jnp.where(low, swap_halves(q), k).astype(bf16)

    ids = ids_ref[...]
    mine = (lax.broadcasted_iota(jnp.int32, (n, tokens), 0) == ids).astype(f32)
    earlier = (
        lax.broadcasted_iota(jnp.int32, (tokens, tokens), 0)
        < lax.broadcasted_iota(jnp.int32, (tokens, tokens), 1)
    ).astype(bf16)
    rank = jnp.sum(dot(mine.astype(bf16), earlier) * mine, axis=0, keepdims=True)
    places = ids.astype(f32) * slot + rank
    send_place[...] = places

    pl.semaphore_wait(barrier, n - 1)

    for d in range(1, n):
        remote(send_place, got_place.at[d], 0, 0, across(d))
    scatter(send_qk, got_qk, 1, (2, 1))
    got_place[0] = places

    def fold(index, send):
        for one, two, cols in pairs:
            top = rows_ref[index, :half, cols].astype(f32)
            bottom = rows_ref[index, half:, cols].astype(f32)
            send[one] = jnp.where(low_half, top, swap_halves(bottom)).astype(bf16)
            send[two] = jnp.where(low_half, swap_halves(top), bottom).astype(bf16)

    loads[4].wait()
    loads[5].wait()
    fold(2, send_g)
    fold(3, send_v)

    wait_bytes(got_place.at[1:], recv_sem.at[0])
    wait_bytes(got_qk.at[: len(early)], recv_sem.at[1])
    scatter(send_g, got_g, 2, (4, 3))

    lane_of = lax.broadcasted_iota(jnp.int32, (capacity, width), 1)
    slot_of = lax.broadcasted_iota(jnp.int32, (n, capacity), 1)
    row_of = lax.broadcasted_iota(jnp.int32, (n, capacity), 0)
    region_row = lax.broadcasted_iota(jnp.int32, (n, tokens), 0).astype(f32) * slot
    first_slot = row_of.astype(f32) * slot
    filled = jnp.zeros((n, capacity), f32)
    table = jnp.zeros((n, tokens), f32)
    for d in range(n):
        place = jnp.broadcast_to(got_place[d], (n, tokens))
        held = (place >= region_row) & (place < region_row + slot)
        end = jnp.sum(held.astype(f32), axis=1, keepdims=True) + first_slot
        used = (slot_of.astype(f32) < end) & (slot_of.astype(f32) >= first_slot)
        used = jnp.sum(used.astype(f32), axis=0, keepdims=True)
        filled = jnp.where(row_of == d, used, filled)
        table = jnp.where(lax.broadcasted_iota(jnp.int32, (n, tokens), 0) == d, place, table)
    bias_cols = jnp.transpose((filled - 1.0) * 1e30)
    for d in range(n):
        bias[d] = jnp.where(lane_of == head_size, bias_cols[:, d : d + 1], 0.0)
    place_cols = jnp.transpose(table)

    def pick(d):
        rows = lax.broadcasted_iota(jnp.int32, (capacity, tokens), 0).astype(f32)
        return (rows == got_place[d]).astype(bf16)

    mark_one = (lane_of == head_size).astype(f32)

    def place_qk(d):
        placed = dot(pick(d), got_qk[d] if d else send_qk[me])
        key_low = jnp.where(low_cap, swap_halves(placed), bias[d])
        query = jnp.where(low_cap, placed, mark_one)
        region_qk[:, d] = placed.astype(bf16).reshape(n, slot, width)
        region_k[:, d] = key_low.astype(bf16).reshape(n, slot, width)
        region_q[:, d * slot : (d + 1) * slot] = query.astype(bf16).reshape(n, slot, width)

    for d in (0,) + early:
        place_qk(d)
    wait_bytes(got_qk.at[: len(late)], recv_sem.at[2])
    for d in late:
        place_qk(d)

    nb = capacity // 128
    blocks = [slice(b * 128, (b + 1) * 128) for b in range(nb)]

    def score_step(t, carry):
        r, b = t // nb, pl.multiple_of(t % nb * 128, 128)
        scores = lax.dot_general(
            region_k[r].reshape(capacity, width),
            region_q[r, pl.ds(b, 128)],
            CONTRACT_LANES,
            preferred_element_type=f32,
        )
        raw = jnp.exp(scores - jnp.max(scores, axis=0, keepdims=True))
        weights = raw * (1.0 / jnp.sum(raw, axis=0, keepdims=True))
        probs[r, :, pl.ds(b, 128)] = weights
        probs_low[r, :, pl.ds(b, 128)] = weights.astype(bf16)
        return carry

    scatter(send_v, got_v, 3, (5, 5))
    lax.fori_loop(0, n * nb, score_step, 0, unroll=n * nb)

    def unfold(got, send, d):
        folded = (got[d] if d else send[me]).astype(f32)
        return jnp.concatenate([folded, swap_halves(folded)], axis=0).astype(bf16)

    wait_bytes(got_g.at[: len(early)], recv_sem.at[3])
    wait_bytes(got_g.at[: len(late)], recv_sem.at[4])
    for d in range(n):
        placed = dot(pick(d), unfold(got_g, send_g, d))
        region_g[:, d] = placed.astype(bf16).reshape(n, slot, width)

    def value_step(r, carry):
        grads = dot(probs_low[r], region_g[r].reshape(capacity, width))
        out_v[:, r] = grads.astype(bf16).reshape(n, slot, width)
        return carry

    lax.fori_loop(0, n, value_step, 0, unroll=n)

    def put(d, source):
        lanes = lax.broadcasted_iota(jnp.int32, (tokens, capacity), 1).astype(f32)
        rows = (lanes == place_cols[:, d : d + 1]).astype(bf16)
        return dot(rows, source[d].reshape(capacity, width))

    quad = n // 2
    mine_low = me % quad

    def low_xor(a):
        return (a + mine_low) % 2 + (a // 2 + mine_low // 2) % 2 * 2

    far_slots = [quad + low_xor(k) for k in range(quad)]
    far_peers = [k + quad * (1 - bits[2]) for k in range(quad)]
    near = [s + (s - mine_low + quad) // quad for s in range(quad - 1)]
    near_slots = [low_xor(k) for k in near]
    near_peers = [k + quad * bits[2] for k in near]

    def give_back(ret, back, kind, make):
        for slots, peers, made in (
            (far_slots, far_peers, range(quad, n)),
            (near_slots, near_peers, range(quad)),
        ):
            for d in made:
                grads = make(d)
                if d:
                    ret[d] = grads
                else:
                    back[me] = grads
            for d, peer in zip(slots, peers):
                remote(ret.at[d], back.at[me], kind, kind + 2, peer)

    def value_back(d):
        grads = put(d, out_v)
        return jnp.where(low_half, grads[:half], swap_halves(grads[half:])).astype(bf16)

    give_back(ret_v, back_v, 4, value_back)

    wait_bytes(got_v.at[1:], recv_sem.at[5])
    for d in range(n):
        placed = jnp.where(low_cap, dot(pick(d), unfold(got_v, send_v, d)), 0.0)
        region_v[:, d] = placed.astype(bf16).reshape(n, slot, width)

    my_scale = scale_ref[me] * root

    def grad_step(r, carry):
        value_low = region_v[r].reshape(capacity, width)
        g = region_g[r].reshape(capacity, width)
        qk = region_qk[r].reshape(capacity, width)
        value_t = jnp.transpose(value_low.astype(f32))[:head_size].astype(bf16)
        g_t = jnp.transpose(g.astype(f32))[:head_size]
        key_t = jnp.transpose(qk.astype(f32))[head_size:].astype(bf16)
        attended = dot(value_t, probs_low[r])
        delta = jnp.sum(g_t * attended, axis=0, keepdims=True)
        for b in blocks:
            dprobs = lax.dot_general(
                value_low, g[b], CONTRACT_LANES, preferred_element_type=f32
            )
            dscores[r, :, b] = (probs[r, :, b] * (dprobs - delta[:, b])).astype(bf16)
        grads = dot(dscores[r], qk)
        raw_t = dot(key_t, dscores[r]).astype(bf16).astype(f32) * my_scale
        raw = jnp.transpose(jnp.concatenate([raw_t, raw_t], axis=0))
        grads = jnp.where(low_cap, grads, raw)
        out_kq[:, r] = grads.astype(bf16).reshape(n, slot, width)
        return carry

    lax.fori_loop(0, n, grad_step, 0, unroll=n)

    give_back(ret_kq, back_kq, 5, lambda d: put(d, out_kq).astype(bf16))

    wait_bytes(back_v.at[1:], recv_sem.at[6])
    wait_bytes(back_kq.at[1:], recv_sem.at[7])
    for kind, refs in enumerate((got_place, send_qk, send_g, send_v, ret_v, ret_kq)):
        wait_bytes(refs.at[1:], send_sem.at[kind])


def unpack_kernel(n, kq_ref, v_ref, oq_ref, ok_ref, ov_ref):
    tokens, width = kq_ref.shape[1:]
    half = tokens // 2
    f32, bf16 = jnp.float32, jnp.bfloat16
    low = lax.broadcasted_iota(jnp.int32, (tokens, width), 1) < width // 2
    low_half = lax.broadcasted_iota(jnp.int32, (half, width), 1) < width // 2
    for pair in range(n // 2):
        cols = slice(pair * width, (pair + 1) * width)
        kq0, kq1 = kq_ref[2 * pair].astype(f32), kq_ref[2 * pair + 1].astype(f32)
        v0, v1 = v_ref[2 * pair].astype(f32), v_ref[2 * pair + 1].astype(f32)
        ok_ref[:, cols] = jnp.where(low, kq0, swap_halves(kq1)).astype(bf16)
        oq_ref[:, cols] = jnp.where(low, swap_halves(kq0), kq1).astype(bf16)
        ov_ref[:half, cols] = jnp.where(low_half, v0, swap_halves(v1)).astype(bf16)
        ov_ref[half:, cols] = jnp.where(low_half, swap_halves(v0), v1).astype(bf16)


def by_heads(queries, key_rows, value_rows, grad_out, owner_shard, logit_scale):
    n = lax.axis_size("tile")
    tokens, columns = queries.shape
    head_size = columns // n
    capacity = 2 * tokens
    slot = capacity // n
    width = 2 * head_size
    bf16, f32 = jnp.bfloat16, jnp.float32
    vmem = pl.BlockSpec(memory_space=pltpu.VMEM)
    anywhere = pl.BlockSpec(memory_space=pltpu.HBM)
    full = pltpu.VMEM((n, tokens, width), bf16)
    folded = pltpu.VMEM((n, tokens // 2, width), bf16)
    region = pltpu.VMEM((n, n, slot, width), bf16)
    square = (n, capacity, capacity)
    grant = 67043328 - 3 * n * tokens * width - 64 * 1024
    back_kq, back_v = pl.pallas_call(
        functools.partial(exchange_kernel, n, slot, head_size),
        out_shape=(
            pltpu.VMEM((n, tokens, width), bf16),
            pltpu.VMEM((n, tokens // 2, width), bf16),
        ),
        in_specs=[anywhere] * 6,
        out_specs=(vmem, vmem),
        scratch_shapes=[pltpu.VMEM((1, tokens), jnp.int32), pltpu.SMEM((n,), f32)]
        + [pltpu.VMEM((4, tokens, columns), bf16)]
        + [pltpu.VMEM((1, tokens), f32), full, folded, folded]
        + [pltpu.VMEM((n, 1, tokens), f32), full, folded, folded]
        + [pltpu.VMEM((n, capacity, width), bf16), region, region, region, region]
        + [pltpu.VMEM((n, capacity, 128), f32), pltpu.VMEM(square, f32)]
        + [pltpu.VMEM(square, bf16), pltpu.VMEM(square, bf16)]
        + [region, region, folded, full]
        + [pltpu.SemaphoreType.DMA((6,))] * 2
        + [pltpu.SemaphoreType.DMA((8,))],
        compiler_params=pltpu.CompilerParams(
            collective_id=0, has_side_effects=True, vmem_limit_bytes=grant
        ),
    )(owner_shard.reshape(1, tokens), logit_scale, queries, key_rows, value_rows, grad_out)
    out = jax.ShapeDtypeStruct((tokens, columns), bf16)
    return pl.pallas_call(
        functools.partial(unpack_kernel, n),
        out_shape=(out, out, out),
        in_specs=[vmem, vmem],
        out_specs=(vmem, vmem, vmem),
        compiler_params=pltpu.CompilerParams(vmem_limit_bytes=8 * 1024 * 1024),
    )(back_kq, back_v)


def attend_heads(query_heads, key_heads, value_heads, dout_heads, live_rows):
    pair_mask = live_rows[None, :, None] & live_rows[None, None, :]
    scores = jnp.einsum("ihe,jhe->hij", query_heads, key_heads, preferred_element_type=jnp.float32)
    scores = jnp.where(pair_mask, scores, -1e30)
    row_max = jnp.max(scores, axis=2, keepdims=True)
    raw_weights = jnp.where(pair_mask, jnp.exp(scores - row_max), 0.0)
    row_sum = jnp.sum(raw_weights, axis=2, keepdims=True)
    row_sum = jnp.where(live_rows[None, :, None], row_sum, 1.0)
    weights = raw_weights / row_sum
    weights_low = weights.astype(jnp.bfloat16)
    attended = jnp.einsum(
        "hij,jhe->ihe", weights_low, value_heads, preferred_element_type=jnp.float32
    )
    row_delta = jnp.sum(dout_heads.astype(jnp.float32) * attended, axis=2)
    dprobs = jnp.einsum("ihe,jhe->hij", dout_heads, value_heads, preferred_element_type=jnp.float32)
    dscores = (weights * (dprobs - jnp.transpose(row_delta)[:, :, None])).astype(jnp.bfloat16)
    grad_value = jnp.einsum(
        "hij,ihe->jhe", weights_low, dout_heads, preferred_element_type=jnp.float32
    ).astype(jnp.bfloat16)
    grad_key = jnp.einsum(
        "hij,ihe->jhe", dscores, query_heads, preferred_element_type=jnp.float32
    ).astype(jnp.bfloat16)
    grad_raw = jnp.einsum(
        "hij,jhe->ihe", dscores, key_heads, preferred_element_type=jnp.float32
    ).astype(jnp.bfloat16)
    return (grad_raw, grad_key, grad_value)


def attend_items(query_items, key_items, value_items, dout_items, live_rows):
    capacity = query_items.shape[0]
    item_count = query_items.shape[1]
    head_size = query_items.shape[2] // 2
    outputs = ([], [], [])
    for item_index in range(item_count):
        halves = ([], [], [])
        for half_index in range(2):
            lower = half_index * head_size
            upper = lower + head_size
            pieces = attend_heads(
                query_items[:, item_index, lower:upper].reshape(capacity, 1, head_size),
                key_items[:, item_index, lower:upper].reshape(capacity, 1, head_size),
                value_items[:, item_index, lower:upper].reshape(capacity, 1, head_size),
                dout_items[:, item_index, lower:upper].reshape(capacity, 1, head_size),
                live_rows,
            )
            for holder, piece in zip(halves, pieces):
                holder.append(piece.reshape(capacity, head_size))
        for holder, parts_list in zip(outputs, halves):
            holder.append(jnp.concatenate(parts_list, axis=1))
    return tuple((jnp.stack(holder, axis=1) for holder in outputs))


def slot_places(owner_shard, shards, slot):
    one_hot = (owner_shard[:, None] == jnp.arange(shards, dtype=jnp.int32)[None, :]).astype(
        jnp.int32
    )
    before = jnp.cumsum(one_hot, axis=0) - one_hot
    rank = jnp.sum(before * one_hot, axis=1)
    return owner_shard * slot + rank


def by_regions(queries, key_rows, value_rows, grad_out, owner_shard, logit_scale):
    shards = lax.axis_size("tile")
    tok_rows, columns = queries.shape
    heads_here = logit_scale.shape[0]
    head_size = columns // heads_here
    capacity = 2 * tok_rows
    slot = capacity // shards
    pairs = heads_here // 2
    width = 2 * head_size
    slot_index = slot_places(owner_shard, shards, slot)
    scale_cols = jnp.repeat(logit_scale / math.sqrt(head_size), head_size)
    scaled = (queries.astype(jnp.float32) * scale_cols).astype(jnp.bfloat16)

    def spread(source):
        return jnp.zeros((capacity,) + source.shape[1:], source.dtype).at[slot_index].set(source)

    sent_query = spread(scaled)
    sent_key = spread(key_rows)
    sent_value = spread(value_rows)
    sent_dout = spread(grad_out)
    flags = spread(jnp.ones((tok_rows,), jnp.int32))
    got_query, got_key, got_value, got_dout, got_flags = (
        lax.all_to_all(sent_query, "tile", split_axis=0, concat_axis=0, tiled=True),
        lax.all_to_all(sent_key, "tile", split_axis=0, concat_axis=0, tiled=True),
        lax.all_to_all(sent_value, "tile", split_axis=0, concat_axis=0, tiled=True),
        lax.all_to_all(sent_dout, "tile", split_axis=0, concat_axis=0, tiled=True),
        lax.all_to_all(flags, "tile", split_axis=0, concat_axis=0, tiled=True),
    )
    grad_raw, grad_key, grad_value = attend_items(
        got_query.reshape(capacity, pairs, width),
        got_key.reshape(capacity, pairs, width),
        got_value.reshape(capacity, pairs, width),
        got_dout.reshape(capacity, pairs, width),
        got_flags > 0,
    )
    returned = (
        lax.all_to_all(
            grad_raw.reshape(capacity, columns), "tile", split_axis=0, concat_axis=0, tiled=True
        ),
        lax.all_to_all(
            grad_key.reshape(capacity, columns), "tile", split_axis=0, concat_axis=0, tiled=True
        ),
        lax.all_to_all(
            grad_value.reshape(capacity, columns), "tile", split_axis=0, concat_axis=0, tiled=True
        ),
    )
    grad_queries = (returned[0][slot_index].astype(jnp.float32) * scale_cols).astype(jnp.bfloat16)
    return (grad_queries, returned[1][slot_index], returned[2][slot_index])


def local(queries, key_rows, value_rows, grad_out, owner_shard, logit_scale):
    shards = lax.axis_size("tile")
    tokens, columns = queries.shape
    heads_here = logit_scale.shape[0]
    slot = 2 * tokens // shards
    fits = (
        shards == heads_here == 8
        and columns == heads_here * 64
        and slot % 16 == 0
        and (2 * tokens) % 128 == 0
        and tokens % 32 == 0
    )
    plan = by_heads if fits else by_regions
    return plan(queries, key_rows, value_rows, grad_out, owner_shard, logit_scale)


def solution(mesh):
    return jax.shard_map(
        local,
        mesh=mesh,
        in_specs=(
            P(("pages", "tile"), "mp"),
            P(("pages", "tile"), "mp"),
            P(("pages", "tile"), "mp"),
            P(("pages", "tile"), "mp"),
            P(("pages", "tile")),
            P("mp"),
        ),
        out_specs=(
            P(("pages", "tile"), "mp"),
            P(("pages", "tile"), "mp"),
            P(("pages", "tile"), "mp"),
        ),
        check_vma=False,
    )
```

```python
import functools
import math

import jax
import jax.numpy as jnp
from jax import lax
from jax.experimental import pallas as pl
from jax.experimental.pallas import tpu as pltpu
from jax.sharding import PartitionSpec as P

MESH = pl.DeviceIdType.MESH
CONTRACT_LANES = (((1,), (1,)), ((), ()))


def dot(left, right):
    return jnp.dot(left, right, preferred_element_type=jnp.float32)


def swap_halves(tile):
    return pltpu.roll(tile, tile.shape[1] // 2, 1)


def exchange_kernel(
    n,
    slot,
    head_size,
    ids_hbm,
    scale_hbm,
    q_hbm,
    k_hbm,
    v_hbm,
    g_hbm,
    grad_q,
    grad_k,
    grad_v,
    ids_ref,
    scale_ref,
    rows_ref,
    send_place,
    send_qk,
    send_g,
    send_v,
    got_place,
    got_qk,
    got_g,
    got_v,
    region_q,
    region_qk,
    region_k,
    region_g,
    region_v,
    bias,
    probs,
    probs_low,
    dscores,
    out_v,
    out_kq,
    ret_v,
    ret_kq,
    back_v,
    back_kq,
    load_sem,
    send_sem,
    recv_sem,
):
    me = lax.axis_index("tile")
    tokens = send_place.shape[1]
    capacity = n * slot
    width = 2 * head_size
    half = tokens // 2
    f32, bf16 = jnp.float32, jnp.bfloat16
    root = 1.0 / math.sqrt(head_size)

    barrier = pltpu.get_barrier_semaphore()
    for d in range(1, n):
        pl.semaphore_signal(
            barrier, inc=1, device_id={"tile": lax.rem(me + d, n)}, device_id_type=MESH
        )
    loads = [
        pltpu.make_async_copy(src, dst, load_sem.at[i])
        for i, (src, dst) in enumerate(
            (
                (ids_hbm, ids_ref),
                (q_hbm, rows_ref.at[0]),
                (k_hbm, rows_ref.at[1]),
                (scale_hbm, scale_ref),
                (g_hbm, rows_ref.at[2]),
                (v_hbm, rows_ref.at[3]),
            )
        )
    ]
    for load in loads:
        load.start()

    def wait_bytes(refs, sem):
        pltpu.make_async_copy(refs, refs, sem).wait()

    bits = [me % 2, me // 2 % 2, me // 4]

    def across(d):
        flips = [d % 2, d // 2 % 2, d // 4]
        return sum((1 - b if f else b) * 2**i for i, (b, f) in enumerate(zip(bits, flips)))

    inner = (bits[1] + bits[2]) % 2
    early, late = (4, 5), (6, 7, 2, 3, 1)
    steps = list(zip((4, 2, 5, 3, 6, 7, 1), (6, 2, 7, 3, 4, 5, 1)))

    def pick_step(outside, inside):
        return outside + inner * (inside - outside)

    def remote(src, dst, send, recv, peer):
        pltpu.make_async_remote_copy(
            src_ref=src,
            dst_ref=dst,
            send_sem=send_sem.at[send],
            recv_sem=recv_sem.at[recv],
            device_id={"tile": peer},
            device_id_type=MESH,
        ).start()

    def scatter(send, got, kind, groups):
        for a, b in steps:
            d = pick_step(a, b)
            peer = pick_step(across(a), across(b))
            group = pick_step(groups[a in early], groups[b in early])
            remote(send.at[peer], got.at[d], kind, group, peer)

    def low_lanes(rows):
        return lax.broadcasted_iota(jnp.int32, (rows, width), 1) < head_size

    low, low_half, low_cap = low_lanes(tokens), low_lanes(half), low_lanes(capacity)
    pairs = [
        (2 * pair, 2 * pair + 1, slice(pair * width, (pair + 1) * width))
        for pair in range(n // 2)
    ]
    for load in loads[:4]:
        load.wait()
    for one, two, cols in pairs:
        lane_scale = jnp.where(low, scale_ref[one] * root, scale_ref[two] * root)
        q = (rows_ref[0, :, cols].astype(f32) * lane_scale).astype(bf16).astype(f32)
        k = rows_ref[1, :, cols].astype(f32)
        send_qk[one] = jnp.where(low, q, swap_halves(k)).astype(bf16)
        send_qk[two] = jnp.where(low, swap_halves(q), k).astype(bf16)

    ids = ids_ref[...]
    mine = (lax.broadcasted_iota(jnp.int32, (n, tokens), 0) == ids).astype(f32)
    earlier = (
        lax.broadcasted_iota(jnp.int32, (tokens, tokens), 0)
        < lax.broadcasted_iota(jnp.int32, (tokens, tokens), 1)
    ).astype(bf16)
    rank = jnp.sum(dot(mine.astype(bf16), earlier) * mine, axis=0, keepdims=True)
    places = ids.astype(f32) * slot + rank
    send_place[...] = places

    pl.semaphore_wait(barrier, n - 1)

    for d in range(1, n):
        remote(send_place, got_place.at[d], 0, 0, across(d))
    scatter(send_qk, got_qk, 1, (2, 1))
    got_place[0] = places

    def fold(index, send):
        for one, two, cols in pairs:
            top = rows_ref[index, :half, cols].astype(f32)
            bottom = rows_ref[index, half:, cols].astype(f32)
            send[one] = jnp.where(low_half, top, swap_halves(bottom)).astype(bf16)
            send[two] = jnp.where(low_half, swap_halves(top), bottom).astype(bf16)

    loads[4].wait()
    loads[5].wait()
    fold(2, send_g)
    fold(3, send_v)
    scatter(send_g, got_g, 2, (4, 3))
    scatter(send_v, got_v, 3, (5, 5))

    wait_bytes(got_place.at[1:], recv_sem.at[0])
    wait_bytes(got_qk.at[: len(early)], recv_sem.at[1])

    lane_of = lax.broadcasted_iota(jnp.int32, (capacity, width), 1)
    slot_of = lax.broadcasted_iota(jnp.int32, (n, capacity), 1)
    row_of = lax.broadcasted_iota(jnp.int32, (n, capacity), 0)
    region_row = lax.broadcasted_iota(jnp.int32, (n, tokens), 0).astype(f32) * slot
    first_slot = row_of.astype(f32) * slot
    filled = jnp.zeros((n, capacity), f32)
    table = jnp.zeros((n, tokens), f32)
    for d in range(n):
        place = jnp.broadcast_to(got_place[d], (n, tokens))
        held = (place >= region_row) & (place < region_row + slot)
        end = jnp.sum(held.astype(f32), axis=1, keepdims=True) + first_slot
        used = (slot_of.astype(f32) < end) & (slot_of.astype(f32) >= first_slot)
        used = jnp.sum(used.astype(f32), axis=0, keepdims=True)
        filled = jnp.where(row_of == d, used, filled)
        table = jnp.where(lax.broadcasted_iota(jnp.int32, (n, tokens), 0) == d, place, table)
    bias_cols = jnp.transpose((filled - 1.0) * 1e30)
    for d in range(n):
        bias[d] = jnp.where(lane_of == head_size, bias_cols[:, d : d + 1], 0.0)
    place_cols = jnp.transpose(table)

    def pick(d):
        rows = lax.broadcasted_iota(jnp.int32, (capacity, tokens), 0).astype(f32)
        return (rows == got_place[d]).astype(bf16)

    mark_one = (lane_of == head_size).astype(f32)

    def place_qk(d):
        placed = dot(pick(d), got_qk[d] if d else send_qk[me])
        key_low = jnp.where(low_cap, swap_halves(placed), bias[d])
        query = jnp.where(low_cap, placed, mark_one)
        region_qk[:, d] = placed.astype(bf16).reshape(n, slot, width)
        region_k[:, d] = key_low.astype(bf16).reshape(n, slot, width)
        region_q[:, d * slot : (d + 1) * slot] = query.astype(bf16).reshape(n, slot, width)

    for d in (0,) + early:
        place_qk(d)
    wait_bytes(got_qk.at[: len(late)], recv_sem.at[2])
    for d in late:
        place_qk(d)

    nb = capacity // 128
    blocks = [slice(b * 128, (b + 1) * 128) for b in range(nb)]

    def score_step(t, carry):
        r, b = t // nb, pl.multiple_of(t % nb * 128, 128)
        scores = lax.dot_general(
            region_k[r].reshape(capacity, width),
            region_q[r, pl.ds(b, 128)],
            CONTRACT_LANES,
            preferred_element_type=f32,
        )
        raw = jnp.exp(scores - jnp.max(scores, axis=0, keepdims=True))
        weights = raw * (1.0 / jnp.sum(raw, axis=0, keepdims=True))
        probs[r, :, pl.ds(b, 128)] = weights
        probs_low[r, :, pl.ds(b, 128)] = weights.astype(bf16)
        return carry

    lax.fori_loop(0, n * nb, score_step, 0, unroll=n * nb)

    def unfold(got, send, d):
        folded = (got[d] if d else send[me]).astype(f32)
        return jnp.concatenate([folded, swap_halves(folded)], axis=0).astype(bf16)

    wait_bytes(got_g.at[: len(early)], recv_sem.at[3])
    wait_bytes(got_g.at[: len(late)], recv_sem.at[4])
    for d in range(n):
        placed = dot(pick(d), unfold(got_g, send_g, d))
        region_g[:, d] = placed.astype(bf16).reshape(n, slot, width)

    def value_step(r, carry):
        grads = dot(probs_low[r], region_g[r].reshape(capacity, width))
        out_v[:, r] = grads.astype(bf16).reshape(n, slot, width)
        return carry

    lax.fori_loop(0, n, value_step, 0, unroll=n)

    def put(d, source):
        lanes = lax.broadcasted_iota(jnp.int32, (tokens, capacity), 1).astype(f32)
        rows = (lanes == place_cols[:, d : d + 1]).astype(bf16)
        return dot(rows, source[d].reshape(capacity, width))

    quad = n // 2
    mine_low = me % quad

    def low_xor(a):
        return (a + mine_low) % 2 + (a // 2 + mine_low // 2) % 2 * 2

    far_slots = [quad + low_xor(k) for k in range(quad)]
    far_peers = [k + quad * (1 - bits[2]) for k in range(quad)]
    near = [s + (s - mine_low + quad) // quad for s in range(quad - 1)]
    near_slots = [low_xor(k) for k in near]
    near_peers = [k + quad * bits[2] for k in near]

    def give_back(ret, back, kind, group, make):
        for d in range(n):
            grads = make(d)
            if d:
                ret[d] = grads
            else:
                back[me] = grads
        far = [(d, peer, group) for d, peer in zip(far_slots, far_peers)]
        close = [(d, peer, group + 1) for d, peer in zip(near_slots, near_peers)]
        for d, peer, recv in (far[0], far[1], close[0], far[2], close[1], far[3], close[2]):
            remote(ret.at[d], back.at[me], kind, recv, peer)

    def value_back(d):
        grads = put(d, out_v)
        return jnp.where(low_half, grads[:half], swap_halves(grads[half:])).astype(bf16)

    give_back(ret_v, back_v, 4, 6, value_back)

    wait_bytes(got_v.at[1:], recv_sem.at[5])
    for d in range(n):
        placed = jnp.where(low_cap, dot(pick(d), unfold(got_v, send_v, d)), 0.0)
        region_v[:, d] = placed.astype(bf16).reshape(n, slot, width)

    my_scale = scale_ref[me] * root

    def grad_step(r, carry):
        value_low = region_v[r].reshape(capacity, width)
        g = region_g[r].reshape(capacity, width)
        qk = region_qk[r].reshape(capacity, width)
        value_t = jnp.transpose(value_low.astype(f32))[:head_size].astype(bf16)
        g_t = jnp.transpose(g.astype(f32))[:head_size]
        key_t = jnp.transpose(qk.astype(f32))[head_size:].astype(bf16)
        attended = dot(value_t, probs_low[r])
        delta = jnp.sum(g_t * attended, axis=0, keepdims=True)
        dprobs = lax.dot_general(value_low, g, CONTRACT_LANES, preferred_element_type=f32)
        dscores[r] = (probs[r] * (dprobs - delta)).astype(bf16)
        grads = dot(dscores[r], qk)
        raw_t = dot(key_t, dscores[r]).astype(bf16).astype(f32) * my_scale
        raw = jnp.transpose(jnp.concatenate([raw_t, raw_t], axis=0))
        grads = jnp.where(low_cap, grads, raw)
        out_kq[:, r] = grads.astype(bf16).reshape(n, slot, width)
        return carry

    lax.fori_loop(0, n, grad_step, 0, unroll=n)

    give_back(ret_kq, back_kq, 5, 8, lambda d: put(d, out_kq).astype(bf16))

    def unpack(half_of_tiles, unpack_pair):
        for k in range(quad // 2):
            pair = half_of_tiles * (quad // 2) + k
            unpack_pair(2 * pair, pl.ds(pl.multiple_of(pair * width, width), width))

    def unpack_v(one, cols):
        v0, v1 = back_v[one].astype(f32), back_v[one + 1].astype(f32)
        grad_v[:half, cols] = jnp.where(low_half, v0, swap_halves(v1)).astype(bf16)
        grad_v[half:, cols] = jnp.where(low_half, swap_halves(v0), v1).astype(bf16)

    def unpack_kq(one, cols):
        kq0, kq1 = back_kq[one].astype(f32), back_kq[one + 1].astype(f32)
        grad_k[:, cols] = jnp.where(low, kq0, swap_halves(kq1)).astype(bf16)
        grad_q[:, cols] = jnp.where(low, swap_halves(kq0), kq1).astype(bf16)

    wait_bytes(back_v.at[: quad - 1], recv_sem.at[7])
    wait_bytes(back_v.at[:quad], recv_sem.at[6])
    unpack(bits[2], unpack_v)
    unpack(1 - bits[2], unpack_v)
    wait_bytes(back_kq.at[: quad - 1], recv_sem.at[9])
    unpack(bits[2], unpack_kq)
    wait_bytes(back_kq.at[:quad], recv_sem.at[8])
    unpack(1 - bits[2], unpack_kq)
    for kind, refs in enumerate((got_place, send_qk, send_g, send_v, ret_v, ret_kq)):
        wait_bytes(refs.at[1:], send_sem.at[kind])


def store_kernel(q_ref, k_ref, v_ref, oq_hbm, ok_hbm, ov_hbm, sem):
    copies = [
        pltpu.make_async_copy(src, dst, sem.at[i])
        for i, (src, dst) in enumerate(((q_ref, oq_hbm), (k_ref, ok_hbm), (v_ref, ov_hbm)))
    ]
    for copy in copies:
        copy.start()
    for copy in copies:
        copy.wait()


def by_heads(queries, key_rows, value_rows, grad_out, owner_shard, logit_scale):
    n = lax.axis_size("tile")
    tokens, columns = queries.shape
    head_size = columns // n
    capacity = 2 * tokens
    slot = capacity // n
    width = 2 * head_size
    bf16, f32 = jnp.bfloat16, jnp.float32
    vmem = pl.BlockSpec(memory_space=pltpu.VMEM)
    anywhere = pl.BlockSpec(memory_space=pltpu.HBM)
    full = pltpu.VMEM((n, tokens, width), bf16)
    folded = pltpu.VMEM((n, tokens // 2, width), bf16)
    region = pltpu.VMEM((n, n, slot, width), bf16)
    square = (n, capacity, capacity)
    grant = 67043328 - 6 * tokens * columns - 64 * 1024
    grads = pl.pallas_call(
        functools.partial(exchange_kernel, n, slot, head_size),
        out_shape=(pltpu.VMEM((tokens, columns), bf16),) * 3,
        in_specs=[anywhere] * 6,
        out_specs=(vmem, vmem, vmem),
        scratch_shapes=[pltpu.VMEM((1, tokens), jnp.int32), pltpu.SMEM((n,), f32)]
        + [pltpu.VMEM((4, tokens, columns), bf16)]
        + [pltpu.VMEM((1, tokens), f32), full, folded, folded]
        + [pltpu.VMEM((n, 1, tokens), f32), full, folded, folded]
        + [pltpu.VMEM((n, capacity, width), bf16), region, region, region, region]
        + [pltpu.VMEM((n, capacity, 128), f32), pltpu.VMEM(square, f32)]
        + [pltpu.VMEM(square, bf16), pltpu.VMEM(square, bf16)]
        + [region, region, folded, full, folded, full]
        + [pltpu.SemaphoreType.DMA((6,))] * 2
        + [pltpu.SemaphoreType.DMA((10,))],
        compiler_params=pltpu.CompilerParams(
            collective_id=0, has_side_effects=True, vmem_limit_bytes=grant
        ),
    )(owner_shard.reshape(1, tokens), logit_scale, queries, key_rows, value_rows, grad_out)
    out = jax.ShapeDtypeStruct((tokens, columns), bf16)
    return pl.pallas_call(
        store_kernel,
        out_shape=(out, out, out),
        in_specs=[vmem, vmem, vmem],
        out_specs=(anywhere, anywhere, anywhere),
        scratch_shapes=[pltpu.SemaphoreType.DMA((3,))],
        compiler_params=pltpu.CompilerParams(vmem_limit_bytes=1024 * 1024),
    )(*grads)


def attend_heads(query_heads, key_heads, value_heads, dout_heads, live_rows):
    pair_mask = live_rows[None, :, None] & live_rows[None, None, :]
    scores = jnp.einsum("ihe,jhe->hij", query_heads, key_heads, preferred_element_type=jnp.float32)
    scores = jnp.where(pair_mask, scores, -1e30)
    row_max = jnp.max(scores, axis=2, keepdims=True)
    raw_weights = jnp.where(pair_mask, jnp.exp(scores - row_max), 0.0)
    row_sum = jnp.sum(raw_weights, axis=2, keepdims=True)
    row_sum = jnp.where(live_rows[None, :, None], row_sum, 1.0)
    weights = raw_weights / row_sum
    weights_low = weights.astype(jnp.bfloat16)
    attended = jnp.einsum(
        "hij,jhe->ihe", weights_low, value_heads, preferred_element_type=jnp.float32
    )
    row_delta = jnp.sum(dout_heads.astype(jnp.float32) * attended, axis=2)
    dprobs = jnp.einsum("ihe,jhe->hij", dout_heads, value_heads, preferred_element_type=jnp.float32)
    dscores = (weights * (dprobs - jnp.transpose(row_delta)[:, :, None])).astype(jnp.bfloat16)
    grad_value = jnp.einsum(
        "hij,ihe->jhe", weights_low, dout_heads, preferred_element_type=jnp.float32
    ).astype(jnp.bfloat16)
    grad_key = jnp.einsum(
        "hij,ihe->jhe", dscores, query_heads, preferred_element_type=jnp.float32
    ).astype(jnp.bfloat16)
    grad_raw = jnp.einsum(
        "hij,jhe->ihe", dscores, key_heads, preferred_element_type=jnp.float32
    ).astype(jnp.bfloat16)
    return (grad_raw, grad_key, grad_value)


def attend_items(query_items, key_items, value_items, dout_items, live_rows):
    capacity = query_items.shape[0]
    item_count = query_items.shape[1]
    head_size = query_items.shape[2] // 2
    outputs = ([], [], [])
    for item_index in range(item_count):
        halves = ([], [], [])
        for half_index in range(2):
            lower = half_index * head_size
            upper = lower + head_size
            pieces = attend_heads(
                query_items[:, item_index, lower:upper].reshape(capacity, 1, head_size),
                key_items[:, item_index, lower:upper].reshape(capacity, 1, head_size),
                value_items[:, item_index, lower:upper].reshape(capacity, 1, head_size),
                dout_items[:, item_index, lower:upper].reshape(capacity, 1, head_size),
                live_rows,
            )
            for holder, piece in zip(halves, pieces):
                holder.append(piece.reshape(capacity, head_size))
        for holder, parts_list in zip(outputs, halves):
            holder.append(jnp.concatenate(parts_list, axis=1))
    return tuple((jnp.stack(holder, axis=1) for holder in outputs))


def slot_places(owner_shard, shards, slot):
    one_hot = (owner_shard[:, None] == jnp.arange(shards, dtype=jnp.int32)[None, :]).astype(
        jnp.int32
    )
    before = jnp.cumsum(one_hot, axis=0) - one_hot
    rank = jnp.sum(before * one_hot, axis=1)
    return owner_shard * slot + rank


def by_regions(queries, key_rows, value_rows, grad_out, owner_shard, logit_scale):
    shards = lax.axis_size("tile")
    tok_rows, columns = queries.shape
    heads_here = logit_scale.shape[0]
    head_size = columns // heads_here
    capacity = 2 * tok_rows
    slot = capacity // shards
    pairs = heads_here // 2
    width = 2 * head_size
    slot_index = slot_places(owner_shard, shards, slot)
    scale_cols = jnp.repeat(logit_scale / math.sqrt(head_size), head_size)
    scaled = (queries.astype(jnp.float32) * scale_cols).astype(jnp.bfloat16)

    def spread(source):
        return jnp.zeros((capacity,) + source.shape[1:], source.dtype).at[slot_index].set(source)

    sent_query = spread(scaled)
    sent_key = spread(key_rows)
    sent_value = spread(value_rows)
    sent_dout = spread(grad_out)
    flags = spread(jnp.ones((tok_rows,), jnp.int32))
    got_query, got_key, got_value, got_dout, got_flags = (
        lax.all_to_all(sent_query, "tile", split_axis=0, concat_axis=0, tiled=True),
        lax.all_to_all(sent_key, "tile", split_axis=0, concat_axis=0, tiled=True),
        lax.all_to_all(sent_value, "tile", split_axis=0, concat_axis=0, tiled=True),
        lax.all_to_all(sent_dout, "tile", split_axis=0, concat_axis=0, tiled=True),
        lax.all_to_all(flags, "tile", split_axis=0, concat_axis=0, tiled=True),
    )
    grad_raw, grad_key, grad_value = attend_items(
        got_query.reshape(capacity, pairs, width),
        got_key.reshape(capacity, pairs, width),
        got_value.reshape(capacity, pairs, width),
        got_dout.reshape(capacity, pairs, width),
        got_flags > 0,
    )
    returned = (
        lax.all_to_all(
            grad_raw.reshape(capacity, columns), "tile", split_axis=0, concat_axis=0, tiled=True
        ),
        lax.all_to_all(
            grad_key.reshape(capacity, columns), "tile", split_axis=0, concat_axis=0, tiled=True
        ),
        lax.all_to_all(
            grad_value.reshape(capacity, columns), "tile", split_axis=0, concat_axis=0, tiled=True
        ),
    )
    grad_queries = (returned[0][slot_index].astype(jnp.float32) * scale_cols).astype(jnp.bfloat16)
    return (grad_queries, returned[1][slot_index], returned[2][slot_index])


def local(queries, key_rows, value_rows, grad_out, owner_shard, logit_scale):
    shards = lax.axis_size("tile")
    tokens, columns = queries.shape
    heads_here = logit_scale.shape[0]
    slot = 2 * tokens // shards
    fits = (
        shards == heads_here == 8
        and columns == heads_here * 64
        and slot % 16 == 0
        and (2 * tokens) % 128 == 0
        and tokens % 32 == 0
    )
    plan = by_heads if fits else by_regions
    return plan(queries, key_rows, value_rows, grad_out, owner_shard, logit_scale)


def solution(mesh):
    return jax.shard_map(
        local,
        mesh=mesh,
        in_specs=(
            P(("pages", "tile"), "mp"),
            P(("pages", "tile"), "mp"),
            P(("pages", "tile"), "mp"),
            P(("pages", "tile"), "mp"),
            P(("pages", "tile")),
            P("mp"),
        ),
        out_specs=(
            P(("pages", "tile"), "mp"),
            P(("pages", "tile"), "mp"),
            P(("pages", "tile"), "mp"),
        ),
        check_vma=False,
    )
```

```python
import functools
import math

import jax
import jax.numpy as jnp
from jax import lax
from jax.experimental import pallas as pl
from jax.experimental.pallas import tpu as pltpu
from jax.sharding import PartitionSpec as P

MESH = pl.DeviceIdType.MESH
CONTRACT_LANES = (((1,), (1,)), ((), ()))


def dot(left, right):
    return jnp.dot(left, right, preferred_element_type=jnp.float32)


def swap_halves(tile):
    return pltpu.roll(tile, tile.shape[1] // 2, 1)


def exchange_kernel(
    n,
    slot,
    head_size,
    ids_hbm,
    scale_hbm,
    q_hbm,
    k_hbm,
    v_hbm,
    g_hbm,
    grad_q,
    grad_k,
    grad_v,
    ids_ref,
    scale_ref,
    rows_ref,
    send_place,
    send_qk,
    send_g,
    send_v,
    got_place,
    got_qk,
    got_g,
    got_v,
    region_q,
    region_qk,
    region_k,
    region_g,
    region_v,
    bias,
    probs,
    probs_low,
    dscores,
    out_v,
    out_kq,
    ret_v,
    ret_kq,
    back_v,
    back_kq,
    load_sem,
    send_sem,
    recv_sem,
):
    me = lax.axis_index("tile")
    tokens = send_place.shape[1]
    capacity = n * slot
    width = 2 * head_size
    half = tokens // 2
    f32, bf16 = jnp.float32, jnp.bfloat16
    root = 1.0 / math.sqrt(head_size)

    barrier = pltpu.get_barrier_semaphore()
    for d in range(1, n):
        pl.semaphore_signal(
            barrier, inc=1, device_id={"tile": lax.rem(me + d, n)}, device_id_type=MESH
        )
    pltpu.make_async_copy(ids_hbm, ids_ref, load_sem.at[0]).start()
    for p in range(4):
        part = pl.ds(p * (tokens // 4), tokens // 4)
        pltpu.make_async_copy(q_hbm.at[part], rows_ref.at[0, part], load_sem.at[1]).start()
        pltpu.make_async_copy(k_hbm.at[part], rows_ref.at[1, part], load_sem.at[1]).start()
    pltpu.make_async_copy(scale_hbm, scale_ref, load_sem.at[2]).start()

    def wait_bytes(refs, sem):
        pltpu.make_async_copy(refs, refs, sem).wait()

    bits = [me % 2, me // 2 % 2, me // 4]

    def across(d):
        flips = [d % 2, d // 2 % 2, d // 4]
        return sum((1 - b if f else b) * 2**i for i, (b, f) in enumerate(zip(bits, flips)))

    inner = (bits[1] + bits[2]) % 2
    early, late = (4, 5), (6, 7, 2, 3, 1)
    steps = list(zip((4, 2, 5, 3, 6, 7, 1), (6, 2, 7, 3, 4, 5, 1)))

    def pick_step(outside, inside):
        return outside + inner * (inside - outside)

    def remote(src, dst, send, recv, peer):
        pltpu.make_async_remote_copy(
            src_ref=src,
            dst_ref=dst,
            send_sem=send_sem.at[send],
            recv_sem=recv_sem.at[recv],
            device_id={"tile": peer},
            device_id_type=MESH,
        ).start()

    def scatter(send, got, kind, groups):
        for a, b in steps:
            d = pick_step(a, b)
            peer = pick_step(across(a), across(b))
            group = pick_step(groups[a in early], groups[b in early])
            remote(send.at[peer], got.at[d], kind, group, peer)

    def low_lanes(rows):
        return lax.broadcasted_iota(jnp.int32, (rows, width), 1) < head_size

    low, low_half, low_cap = low_lanes(tokens), low_lanes(half), low_lanes(capacity)
    pairs = [
        (2 * pair, 2 * pair + 1, slice(pair * width, (pair + 1) * width))
        for pair in range(n // 2)
    ]
    pltpu.make_async_copy(ids_hbm, ids_ref, load_sem.at[0]).wait()
    wait_bytes(rows_ref.at[:2], load_sem.at[1])
    pltpu.make_async_copy(scale_hbm, scale_ref, load_sem.at[2]).wait()
    pltpu.make_async_copy(g_hbm, rows_ref.at[2], load_sem.at[3]).start()
    pltpu.make_async_copy(v_hbm, rows_ref.at[3], load_sem.at[3]).start()
    for one, two, cols in pairs:
        lane_scale = jnp.where(low, scale_ref[one] * root, scale_ref[two] * root)
        q = (rows_ref[0, :, cols].astype(f32) * lane_scale).astype(bf16).astype(f32)
        k = rows_ref[1, :, cols].astype(f32)
        send_qk[one] = jnp.where(low, q, swap_halves(k)).astype(bf16)
        send_qk[two] = jnp.where(low, swap_halves(q), k).astype(bf16)

    ids = ids_ref[...]
    mine = (lax.broadcasted_iota(jnp.int32, (n, tokens), 0) == ids).astype(f32)
    earlier = (
        lax.broadcasted_iota(jnp.int32, (tokens, tokens), 0)
        < lax.broadcasted_iota(jnp.int32, (tokens, tokens), 1)
    ).astype(bf16)
    rank = jnp.sum(dot(mine.astype(bf16), earlier) * mine, axis=0, keepdims=True)
    places = ids.astype(f32) * slot + rank
    send_place[...] = places

    pl.semaphore_wait(barrier, n - 1)

    for d in range(1, n):
        remote(send_place, got_place.at[d], 0, 0, across(d))
    scatter(send_qk, got_qk, 1, (2, 1))
    got_place[0] = places

    def fold(index, send):
        for one, two, cols in pairs:
            top = rows_ref[index, :half, cols].astype(f32)
            bottom = rows_ref[index, half:, cols].astype(f32)
            send[one] = jnp.where(low_half, top, swap_halves(bottom)).astype(bf16)
            send[two] = jnp.where(low_half, swap_halves(top), bottom).astype(bf16)

    wait_bytes(rows_ref.at[2:], load_sem.at[3])
    fold(2, send_g)
    fold(3, send_v)
    scatter(send_g, got_g, 2, (4, 3))
    scatter(send_v, got_v, 3, (5, 5))

    wait_bytes(got_place.at[1:], recv_sem.at[0])

    lane_of = lax.broadcasted_iota(jnp.int32, (capacity, width), 1)
    slot_of = lax.broadcasted_iota(jnp.int32, (n, capacity), 1)
    row_of = lax.broadcasted_iota(jnp.int32, (n, capacity), 0)
    region_row = lax.broadcasted_iota(jnp.int32, (n, tokens), 0).astype(f32) * slot
    first_slot = row_of.astype(f32) * slot
    filled = jnp.zeros((n, capacity), f32)
    table = jnp.zeros((n, tokens), f32)
    for d in range(n):
        place = jnp.broadcast_to(got_place[d], (n, tokens))
        held = (place >= region_row) & (place < region_row + slot)
        end = jnp.sum(held.astype(f32), axis=1, keepdims=True) + first_slot
        used = (slot_of.astype(f32) < end) & (slot_of.astype(f32) >= first_slot)
        used = jnp.sum(used.astype(f32), axis=0, keepdims=True)
        filled = jnp.where(row_of == d, used, filled)
        table = jnp.where(lax.broadcasted_iota(jnp.int32, (n, tokens), 0) == d, place, table)
    bias_cols = jnp.transpose((filled - 1.0) * 1e30)
    for d in range(n):
        bias[d] = jnp.where(lane_of == head_size, bias_cols[:, d : d + 1], 0.0)
    place_cols = jnp.transpose(table)

    def pick(d):
        rows = lax.broadcasted_iota(jnp.int32, (capacity, tokens), 0).astype(f32)
        return (rows == got_place[d]).astype(bf16)

    mark_one = (lane_of == head_size).astype(f32)

    def place_qk(d):
        placed = dot(pick(d), got_qk[d] if d else send_qk[me])
        key_low = jnp.where(low_cap, swap_halves(placed), bias[d])
        query = jnp.where(low_cap, placed, mark_one)
        region_qk[:, d] = placed.astype(bf16).reshape(n, slot, width)
        region_k[:, d] = key_low.astype(bf16).reshape(n, slot, width)
        region_q[:, d * slot : (d + 1) * slot] = query.astype(bf16).reshape(n, slot, width)

    wait_bytes(got_qk.at[: len(late)], recv_sem.at[2])
    for d in (0,) + late:
        place_qk(d)
    wait_bytes(got_qk.at[: len(early)], recv_sem.at[1])
    for d in early:
        place_qk(d)

    nb = capacity // 128
    blocks = [slice(b * 128, (b + 1) * 128) for b in range(nb)]

    def score_step(t, carry):
        r, b = t // nb, pl.multiple_of(t % nb * 128, 128)
        scores = lax.dot_general(
            region_k[r].reshape(capacity, width),
            region_q[r, pl.ds(b, 128)],
            CONTRACT_LANES,
            preferred_element_type=f32,
        )
        raw = jnp.exp(scores - jnp.max(scores, axis=0, keepdims=True))
        weights = raw * (1.0 / jnp.sum(raw, axis=0, keepdims=True))
        probs[r, :, pl.ds(b, 128)] = weights
        probs_low[r, :, pl.ds(b, 128)] = weights.astype(bf16)
        return carry

    lax.fori_loop(0, n * nb, score_step, 0, unroll=n * nb)

    def unfold(got, send, d):
        folded = (got[d] if d else send[me]).astype(f32)
        return jnp.concatenate([folded, swap_halves(folded)], axis=0).astype(bf16)

    def place_g(slots):
        for d in slots:
            placed = dot(pick(d), unfold(got_g, send_g, d))
            region_g[:, d] = placed.astype(bf16).reshape(n, slot, width)

    wait_bytes(got_g.at[: len(late)], recv_sem.at[4])
    place_g((0,) + late)
    wait_bytes(got_g.at[: len(early)], recv_sem.at[3])
    place_g(early)

    def value_step(r, carry):
        grads = dot(probs_low[r], region_g[r].reshape(capacity, width))
        out_v[:, r] = grads.astype(bf16).reshape(n, slot, width)
        return carry

    lax.fori_loop(0, n, value_step, 0, unroll=n)

    def put(d, source):
        lanes = lax.broadcasted_iota(jnp.int32, (tokens, capacity), 1).astype(f32)
        rows = (lanes == place_cols[:, d : d + 1]).astype(bf16)
        return dot(rows, source[d].reshape(capacity, width))

    quad = n // 2
    mine_low = me % quad

    def low_xor(a):
        return (a + mine_low) % 2 + (a // 2 + mine_low // 2) % 2 * 2

    far_slots = [quad + low_xor(k) for k in range(quad)]
    far_peers = [k + quad * (1 - bits[2]) for k in range(quad)]
    near = [s + (s - mine_low + quad) // quad for s in range(quad - 1)]
    near_slots = [low_xor(k) for k in near]
    near_peers = [k + quad * bits[2] for k in near]

    def give_back(ret, back, kind, group, make):
        for d in range(n):
            grads = make(d)
            if d:
                ret[d] = grads
            else:
                back[me] = grads
        far = [(d, peer, group) for d, peer in zip(far_slots, far_peers)]
        close = [(d, peer, group + 1) for d, peer in zip(near_slots, near_peers)]
        for d, peer, recv in (far[0], far[1], close[0], far[2], close[1], far[3], close[2]):
            remote(ret.at[d], back.at[me], kind, recv, peer)

    def value_back(d):
        grads = put(d, out_v)
        return jnp.where(low_half, grads[:half], swap_halves(grads[half:])).astype(bf16)

    give_back(ret_v, back_v, 4, 6, value_back)

    wait_bytes(got_v.at[1:], recv_sem.at[5])
    for d in range(n):
        placed = jnp.where(low_cap, dot(pick(d), unfold(got_v, send_v, d)), 0.0)
        region_v[:, d] = placed.astype(bf16).reshape(n, slot, width)

    my_scale = scale_ref[me] * root

    def grad_step(r, carry):
        value_low = region_v[r].reshape(capacity, width)
        g = region_g[r].reshape(capacity, width)
        qk = region_qk[r].reshape(capacity, width)
        value_t = jnp.transpose(value_low.astype(f32))[:head_size].astype(bf16)
        g_t = jnp.transpose(g.astype(f32))[:head_size]
        key_t = jnp.transpose(qk.astype(f32))[head_size:].astype(bf16)
        attended = dot(value_t, probs_low[r])
        delta = jnp.sum(g_t * attended, axis=0, keepdims=True)
        dprobs = lax.dot_general(value_low, g, CONTRACT_LANES, preferred_element_type=f32)
        dscores[r] = (probs[r] * (dprobs - delta)).astype(bf16)
        grads = dot(dscores[r], qk)
        raw_t = dot(key_t, dscores[r]).astype(bf16).astype(f32) * my_scale
        raw = jnp.transpose(jnp.concatenate([raw_t, raw_t], axis=0))
        grads = jnp.where(low_cap, grads, raw)
        out_kq[:, r] = grads.astype(bf16).reshape(n, slot, width)
        return carry

    lax.fori_loop(0, n, grad_step, 0, unroll=n)

    give_back(ret_kq, back_kq, 5, 8, lambda d: put(d, out_kq).astype(bf16))

    def unpack(half_of_tiles, unpack_pair):
        for k in range(quad // 2):
            pair = half_of_tiles * (quad // 2) + k
            unpack_pair(2 * pair, pl.ds(pl.multiple_of(pair * width, width), width))

    def unpack_v(one, cols):
        v0, v1 = back_v[one].astype(f32), back_v[one + 1].astype(f32)
        grad_v[:half, cols] = jnp.where(low_half, v0, swap_halves(v1)).astype(bf16)
        grad_v[half:, cols] = jnp.where(low_half, swap_halves(v0), v1).astype(bf16)

    def unpack_kq(one, cols):
        kq0, kq1 = back_kq[one].astype(f32), back_kq[one + 1].astype(f32)
        grad_k[:, cols] = jnp.where(low, kq0, swap_halves(kq1)).astype(bf16)
        grad_q[:, cols] = jnp.where(low, swap_halves(kq0), kq1).astype(bf16)

    wait_bytes(back_v.at[: quad - 1], recv_sem.at[7])
    wait_bytes(back_v.at[:quad], recv_sem.at[6])
    unpack(bits[2], unpack_v)
    unpack(1 - bits[2], unpack_v)
    wait_bytes(back_kq.at[: quad - 1], recv_sem.at[9])
    unpack(bits[2], unpack_kq)
    wait_bytes(back_kq.at[:quad], recv_sem.at[8])
    unpack(1 - bits[2], unpack_kq)
    for kind, refs in enumerate((got_place, send_qk, send_g, send_v, ret_v, ret_kq)):
        wait_bytes(refs.at[1:], send_sem.at[kind])


def store_kernel(q_ref, k_ref, v_ref, oq_hbm, ok_hbm, ov_hbm, sem):
    pieces = 4
    rows = q_ref.shape[0] // pieces
    pairs = ((q_ref, oq_hbm), (k_ref, ok_hbm), (v_ref, ov_hbm))
    for p in range(pieces):
        for i, (src, dst) in enumerate(pairs):
            part = slice(p * rows, (p + 1) * rows)
            pltpu.make_async_copy(src.at[part], dst.at[part], sem.at[i]).start()
    for i, (src, dst) in enumerate(pairs):
        pltpu.make_async_copy(src, dst, sem.at[i]).wait()


def by_heads(queries, key_rows, value_rows, grad_out, owner_shard, logit_scale):
    n = lax.axis_size("tile")
    tokens, columns = queries.shape
    head_size = columns // n
    capacity = 2 * tokens
    slot = capacity // n
    width = 2 * head_size
    bf16, f32 = jnp.bfloat16, jnp.float32
    vmem = pl.BlockSpec(memory_space=pltpu.VMEM)
    anywhere = pl.BlockSpec(memory_space=pltpu.HBM)
    full = pltpu.VMEM((n, tokens, width), bf16)
    folded = pltpu.VMEM((n, tokens // 2, width), bf16)
    region = pltpu.VMEM((n, n, slot, width), bf16)
    square = (n, capacity, capacity)
    grant = 67043328 - 6 * tokens * columns - 64 * 1024
    grads = pl.pallas_call(
        functools.partial(exchange_kernel, n, slot, head_size),
        out_shape=(pltpu.VMEM((tokens, columns), bf16),) * 3,
        in_specs=[anywhere] * 6,
        out_specs=(vmem, vmem, vmem),
        scratch_shapes=[pltpu.VMEM((1, tokens), jnp.int32), pltpu.SMEM((n,), f32)]
        + [pltpu.VMEM((4, tokens, columns), bf16)]
        + [pltpu.VMEM((1, tokens), f32), full, folded, folded]
        + [pltpu.VMEM((n, 1, tokens), f32), full, folded, folded]
        + [pltpu.VMEM((n, capacity, width), bf16), region, region, region, region]
        + [pltpu.VMEM((n, capacity, 128), f32), pltpu.VMEM(square, f32)]
        + [pltpu.VMEM(square, bf16), pltpu.VMEM(square, bf16)]
        + [region, region, folded, full, folded, full]
        + [pltpu.SemaphoreType.DMA((4,)), pltpu.SemaphoreType.DMA((6,))]
        + [pltpu.SemaphoreType.DMA((10,))],
        compiler_params=pltpu.CompilerParams(
            collective_id=0, has_side_effects=True, vmem_limit_bytes=grant
        ),
    )(owner_shard.reshape(1, tokens), logit_scale, queries, key_rows, value_rows, grad_out)
    out = jax.ShapeDtypeStruct((tokens, columns), bf16)
    return pl.pallas_call(
        store_kernel,
        out_shape=(out, out, out),
        in_specs=[vmem, vmem, vmem],
        out_specs=(anywhere, anywhere, anywhere),
        scratch_shapes=[pltpu.SemaphoreType.DMA((3,))],
        compiler_params=pltpu.CompilerParams(vmem_limit_bytes=1024 * 1024),
    )(*grads)


def attend_heads(query_heads, key_heads, value_heads, dout_heads, live_rows):
    pair_mask = live_rows[None, :, None] & live_rows[None, None, :]
    scores = jnp.einsum("ihe,jhe->hij", query_heads, key_heads, preferred_element_type=jnp.float32)
    scores = jnp.where(pair_mask, scores, -1e30)
    row_max = jnp.max(scores, axis=2, keepdims=True)
    raw_weights = jnp.where(pair_mask, jnp.exp(scores - row_max), 0.0)
    row_sum = jnp.sum(raw_weights, axis=2, keepdims=True)
    row_sum = jnp.where(live_rows[None, :, None], row_sum, 1.0)
    weights = raw_weights / row_sum
    weights_low = weights.astype(jnp.bfloat16)
    attended = jnp.einsum(
        "hij,jhe->ihe", weights_low, value_heads, preferred_element_type=jnp.float32
    )
    row_delta = jnp.sum(dout_heads.astype(jnp.float32) * attended, axis=2)
    dprobs = jnp.einsum("ihe,jhe->hij", dout_heads, value_heads, preferred_element_type=jnp.float32)
    dscores = (weights * (dprobs - jnp.transpose(row_delta)[:, :, None])).astype(jnp.bfloat16)
    grad_value = jnp.einsum(
        "hij,ihe->jhe", weights_low, dout_heads, preferred_element_type=jnp.float32
    ).astype(jnp.bfloat16)
    grad_key = jnp.einsum(
        "hij,ihe->jhe", dscores, query_heads, preferred_element_type=jnp.float32
    ).astype(jnp.bfloat16)
    grad_raw = jnp.einsum(
        "hij,jhe->ihe", dscores, key_heads, preferred_element_type=jnp.float32
    ).astype(jnp.bfloat16)
    return (grad_raw, grad_key, grad_value)


def attend_items(query_items, key_items, value_items, dout_items, live_rows):
    capacity = query_items.shape[0]
    item_count = query_items.shape[1]
    head_size = query_items.shape[2] // 2
    outputs = ([], [], [])
    for item_index in range(item_count):
        halves = ([], [], [])
        for half_index in range(2):
            lower = half_index * head_size
            upper = lower + head_size
            pieces = attend_heads(
                query_items[:, item_index, lower:upper].reshape(capacity, 1, head_size),
                key_items[:, item_index, lower:upper].reshape(capacity, 1, head_size),
                value_items[:, item_index, lower:upper].reshape(capacity, 1, head_size),
                dout_items[:, item_index, lower:upper].reshape(capacity, 1, head_size),
                live_rows,
            )
            for holder, piece in zip(halves, pieces):
                holder.append(piece.reshape(capacity, head_size))
        for holder, parts_list in zip(outputs, halves):
            holder.append(jnp.concatenate(parts_list, axis=1))
    return tuple((jnp.stack(holder, axis=1) for holder in outputs))


def slot_places(owner_shard, shards, slot):
    one_hot = (owner_shard[:, None] == jnp.arange(shards, dtype=jnp.int32)[None, :]).astype(
        jnp.int32
    )
    before = jnp.cumsum(one_hot, axis=0) - one_hot
    rank = jnp.sum(before * one_hot, axis=1)
    return owner_shard * slot + rank


def by_regions(queries, key_rows, value_rows, grad_out, owner_shard, logit_scale):
    shards = lax.axis_size("tile")
    tok_rows, columns = queries.shape
    heads_here = logit_scale.shape[0]
    head_size = columns // heads_here
    capacity = 2 * tok_rows
    slot = capacity // shards
    pairs = heads_here // 2
    width = 2 * head_size
    slot_index = slot_places(owner_shard, shards, slot)
    scale_cols = jnp.repeat(logit_scale / math.sqrt(head_size), head_size)
    scaled = (queries.astype(jnp.float32) * scale_cols).astype(jnp.bfloat16)

    def spread(source):
        return jnp.zeros((capacity,) + source.shape[1:], source.dtype).at[slot_index].set(source)

    sent_query = spread(scaled)
    sent_key = spread(key_rows)
    sent_value = spread(value_rows)
    sent_dout = spread(grad_out)
    flags = spread(jnp.ones((tok_rows,), jnp.int32))
    got_query, got_key, got_value, got_dout, got_flags = (
        lax.all_to_all(sent_query, "tile", split_axis=0, concat_axis=0, tiled=True),
        lax.all_to_all(sent_key, "tile", split_axis=0, concat_axis=0, tiled=True),
        lax.all_to_all(sent_value, "tile", split_axis=0, concat_axis=0, tiled=True),
        lax.all_to_all(sent_dout, "tile", split_axis=0, concat_axis=0, tiled=True),
        lax.all_to_all(flags, "tile", split_axis=0, concat_axis=0, tiled=True),
    )
    grad_raw, grad_key, grad_value = attend_items(
        got_query.reshape(capacity, pairs, width),
        got_key.reshape(capacity, pairs, width),
        got_value.reshape(capacity, pairs, width),
        got_dout.reshape(capacity, pairs, width),
        got_flags > 0,
    )
    returned = (
        lax.all_to_all(
            grad_raw.reshape(capacity, columns), "tile", split_axis=0, concat_axis=0, tiled=True
        ),
        lax.all_to_all(
            grad_key.reshape(capacity, columns), "tile", split_axis=0, concat_axis=0, tiled=True
        ),
        lax.all_to_all(
            grad_value.reshape(capacity, columns), "tile", split_axis=0, concat_axis=0, tiled=True
        ),
    )
    grad_queries = (returned[0][slot_index].astype(jnp.float32) * scale_cols).astype(jnp.bfloat16)
    return (grad_queries, returned[1][slot_index], returned[2][slot_index])


def local(queries, key_rows, value_rows, grad_out, owner_shard, logit_scale):
    shards = lax.axis_size("tile")
    tokens, columns = queries.shape
    heads_here = logit_scale.shape[0]
    slot = 2 * tokens // shards
    fits = (
        shards == heads_here == 8
        and columns == heads_here * 64
        and slot % 16 == 0
        and (2 * tokens) % 128 == 0
        and tokens % 32 == 0
    )
    plan = by_heads if fits else by_regions
    return plan(queries, key_rows, value_rows, grad_out, owner_shard, logit_scale)


def solution(mesh):
    return jax.shard_map(
        local,
        mesh=mesh,
        in_specs=(
            P(("pages", "tile"), "mp"),
            P(("pages", "tile"), "mp"),
            P(("pages", "tile"), "mp"),
            P(("pages", "tile"), "mp"),
            P(("pages", "tile")),
            P("mp"),
        ),
        out_specs=(
            P(("pages", "tile"), "mp"),
            P(("pages", "tile"), "mp"),
            P(("pages", "tile"), "mp"),
        ),
        check_vma=False,
    )
```

```python
import functools
import math

import jax
import jax.numpy as jnp
from jax import lax
from jax.experimental import pallas as pl
from jax.experimental.pallas import tpu as pltpu
from jax.sharding import PartitionSpec as P

MESH = pl.DeviceIdType.MESH
CONTRACT_LANES = (((1,), (1,)), ((), ()))


def dot(left, right):
    return jnp.dot(left, right, preferred_element_type=jnp.float32)


def swap_halves(tile):
    return pltpu.roll(tile, tile.shape[1] // 2, 1)


def exchange_kernel(
    n,
    slot,
    head_size,
    ids_hbm,
    scale_hbm,
    q_hbm,
    k_hbm,
    v_hbm,
    g_hbm,
    grad_q,
    grad_k,
    grad_v,
    ids_ref,
    scale_ref,
    rows_ref,
    send_place,
    send_qk,
    send_g,
    send_v,
    got_place,
    got_qk,
    got_g,
    got_v,
    region_q,
    region_qk,
    region_k,
    region_g,
    region_v,
    bias,
    probs,
    probs_low,
    dscores,
    out_v,
    out_kq,
    ret_v,
    ret_kq,
    back_v,
    back_kq,
    load_sem,
    send_sem,
    recv_sem,
):
    me = lax.axis_index("tile")
    tokens = send_place.shape[1]
    capacity = n * slot
    width = 2 * head_size
    half = tokens // 2
    f32, bf16 = jnp.float32, jnp.bfloat16
    root = 1.0 / math.sqrt(head_size)

    barrier = pltpu.get_barrier_semaphore()
    for d in range(1, n):
        pl.semaphore_signal(
            barrier, inc=1, device_id={"tile": lax.rem(me + d, n)}, device_id_type=MESH
        )
    pltpu.make_async_copy(ids_hbm, ids_ref, load_sem.at[0]).start()
    for p in range(4):
        part = pl.ds(p * (tokens // 4), tokens // 4)
        pltpu.make_async_copy(q_hbm.at[part], rows_ref.at[0, part], load_sem.at[1]).start()
        pltpu.make_async_copy(k_hbm.at[part], rows_ref.at[1, part], load_sem.at[1]).start()
    pltpu.make_async_copy(scale_hbm, scale_ref, load_sem.at[2]).start()

    def wait_bytes(refs, sem):
        pltpu.make_async_copy(refs, refs, sem).wait()

    bits = [me % 2, me // 2 % 2, me // 4]

    def across(d):
        flips = [d % 2, d // 2 % 2, d // 4]
        return sum((1 - b if f else b) * 2**i for i, (b, f) in enumerate(zip(bits, flips)))

    inner = (bits[1] + bits[2]) % 2
    early, late = (4, 5), (6, 7, 2, 3, 1)
    steps = list(zip((4, 2, 5, 3, 6, 7, 1), (6, 2, 7, 3, 4, 5, 1)))

    def pick_step(outside, inside):
        return outside + inner * (inside - outside)

    def remote(src, dst, send, recv, peer):
        pltpu.make_async_remote_copy(
            src_ref=src,
            dst_ref=dst,
            send_sem=send_sem.at[send],
            recv_sem=recv_sem.at[recv],
            device_id={"tile": peer},
            device_id_type=MESH,
        ).start()

    def scatter(send, got, kind, groups):
        for a, b in steps:
            d = pick_step(a, b)
            peer = pick_step(across(a), across(b))
            group = pick_step(groups[a in early], groups[b in early])
            remote(send.at[peer], got.at[d], kind, group, peer)

    def low_lanes(rows):
        return lax.broadcasted_iota(jnp.int32, (rows, width), 1) < head_size

    low, low_half, low_cap = low_lanes(tokens), low_lanes(half), low_lanes(capacity)
    pairs = [
        (2 * pair, 2 * pair + 1, slice(pair * width, (pair + 1) * width))
        for pair in range(n // 2)
    ]
    pltpu.make_async_copy(ids_hbm, ids_ref, load_sem.at[0]).wait()
    wait_bytes(rows_ref.at[:2], load_sem.at[1])
    pltpu.make_async_copy(scale_hbm, scale_ref, load_sem.at[2]).wait()
    pltpu.make_async_copy(g_hbm, rows_ref.at[2], load_sem.at[3]).start()
    pltpu.make_async_copy(v_hbm, rows_ref.at[3], load_sem.at[3]).start()
    for one, two, cols in pairs:
        lane_scale = jnp.where(low, scale_ref[one] * root, scale_ref[two] * root)
        q = (rows_ref[0, :, cols].astype(f32) * lane_scale).astype(bf16).astype(f32)
        k = rows_ref[1, :, cols].astype(f32)
        send_qk[one] = jnp.where(low, q, swap_halves(k)).astype(bf16)
        send_qk[two] = jnp.where(low, swap_halves(q), k).astype(bf16)

    ids = ids_ref[...]
    mine = (lax.broadcasted_iota(jnp.int32, (n, tokens), 0) == ids).astype(f32)
    earlier = (
        lax.broadcasted_iota(jnp.int32, (tokens, tokens), 0)
        < lax.broadcasted_iota(jnp.int32, (tokens, tokens), 1)
    ).astype(bf16)
    rank = jnp.sum(dot(mine.astype(bf16), earlier) * mine, axis=0, keepdims=True)
    places = ids.astype(f32) * slot + rank
    send_place[...] = places

    pl.semaphore_wait(barrier, n - 1)

    for d in range(1, n):
        remote(send_place, got_place.at[d], 0, 0, across(d))
    scatter(send_qk, got_qk, 1, (2, 1))
    got_place[0] = places

    def fold(index, send):
        for one, two, cols in pairs:
            top = rows_ref[index, :half, cols].astype(f32)
            bottom = rows_ref[index, half:, cols].astype(f32)
            send[one] = jnp.where(low_half, top, swap_halves(bottom)).astype(bf16)
            send[two] = jnp.where(low_half, swap_halves(top), bottom).astype(bf16)

    wait_bytes(rows_ref.at[2:], load_sem.at[3])
    fold(2, send_g)
    fold(3, send_v)
    second = lax.axis_index("mp")

    def send_rest():
        scatter(send_g, got_g, 2, (4, 3))
        scatter(send_v, got_v, 3, (5, 5))

    pl.when(second == 0)(send_rest)

    wait_bytes(got_place.at[1:], recv_sem.at[0])

    lane_of = lax.broadcasted_iota(jnp.int32, (capacity, width), 1)
    slot_of = lax.broadcasted_iota(jnp.int32, (n, capacity), 1)
    row_of = lax.broadcasted_iota(jnp.int32, (n, capacity), 0)
    region_row = lax.broadcasted_iota(jnp.int32, (n, tokens), 0).astype(f32) * slot
    first_slot = row_of.astype(f32) * slot
    filled = jnp.zeros((n, capacity), f32)
    table = jnp.zeros((n, tokens), f32)
    for d in range(n):
        place = jnp.broadcast_to(got_place[d], (n, tokens))
        held = (place >= region_row) & (place < region_row + slot)
        end = jnp.sum(held.astype(f32), axis=1, keepdims=True) + first_slot
        used = (slot_of.astype(f32) < end) & (slot_of.astype(f32) >= first_slot)
        used = jnp.sum(used.astype(f32), axis=0, keepdims=True)
        filled = jnp.where(row_of == d, used, filled)
        table = jnp.where(lax.broadcasted_iota(jnp.int32, (n, tokens), 0) == d, place, table)
    bias_cols = jnp.transpose((filled - 1.0) * 1e30)
    for d in range(n):
        bias[d] = jnp.where(lane_of == head_size, bias_cols[:, d : d + 1], 0.0)
    place_cols = jnp.transpose(table)

    def pick(d):
        rows = lax.broadcasted_iota(jnp.int32, (capacity, tokens), 0).astype(f32)
        return (rows == got_place[d]).astype(bf16)

    mark_one = (lane_of == head_size).astype(f32)

    def place_qk(d):
        placed = dot(pick(d), got_qk[d] if d else send_qk[me])
        key_low = jnp.where(low_cap, swap_halves(placed), bias[d])
        query = jnp.where(low_cap, placed, mark_one)
        region_qk[:, d] = placed.astype(bf16).reshape(n, slot, width)
        region_k[:, d] = key_low.astype(bf16).reshape(n, slot, width)
        region_q[:, d * slot : (d + 1) * slot] = query.astype(bf16).reshape(n, slot, width)

    wait_bytes(got_qk.at[: len(late)], recv_sem.at[2])
    pl.when(second == 1)(send_rest)
    for d in (0,) + late:
        place_qk(d)
    wait_bytes(got_qk.at[: len(early)], recv_sem.at[1])
    for d in early:
        place_qk(d)

    nb = capacity // 128
    blocks = [slice(b * 128, (b + 1) * 128) for b in range(nb)]

    def score_step(t, carry):
        r, b = t // nb, pl.multiple_of(t % nb * 128, 128)
        scores = lax.dot_general(
            region_k[r].reshape(capacity, width),
            region_q[r, pl.ds(b, 128)],
            CONTRACT_LANES,
            preferred_element_type=f32,
        )
        raw = jnp.exp(scores - jnp.max(scores, axis=0, keepdims=True))
        weights = raw * (1.0 / jnp.sum(raw, axis=0, keepdims=True))
        probs[r, :, pl.ds(b, 128)] = weights
        probs_low[r, :, pl.ds(b, 128)] = weights.astype(bf16)
        return carry

    lax.fori_loop(0, n * nb, score_step, 0, unroll=n * nb)

    def unfold(got, send, d):
        folded = (got[d] if d else send[me]).astype(f32)
        return jnp.concatenate([folded, swap_halves(folded)], axis=0).astype(bf16)

    def place_g(slots):
        for d in slots:
            placed = dot(pick(d), unfold(got_g, send_g, d))
            region_g[:, d] = placed.astype(bf16).reshape(n, slot, width)

    wait_bytes(got_g.at[: len(late)], recv_sem.at[4])
    place_g((0,) + late)
    wait_bytes(got_g.at[: len(early)], recv_sem.at[3])
    place_g(early)

    def value_step(r, carry):
        grads = dot(probs_low[r], region_g[r].reshape(capacity, width))
        out_v[:, r] = grads.astype(bf16).reshape(n, slot, width)
        return carry

    lax.fori_loop(0, n, value_step, 0, unroll=n)

    def put(d, source):
        lanes = lax.broadcasted_iota(jnp.int32, (tokens, capacity), 1).astype(f32)
        rows = (lanes == place_cols[:, d : d + 1]).astype(bf16)
        return dot(rows, source[d].reshape(capacity, width))

    quad = n // 2
    mine_low = me % quad

    def low_xor(a):
        return (a + mine_low) % 2 + (a // 2 + mine_low // 2) % 2 * 2

    far_slots = [quad + low_xor(k) for k in range(quad)]
    far_peers = [k + quad * (1 - bits[2]) for k in range(quad)]
    near = [s + (s - mine_low + quad) // quad for s in range(quad - 1)]
    near_slots = [low_xor(k) for k in near]
    near_peers = [k + quad * bits[2] for k in near]

    def give_back(ret, back, kind, group, make):
        for d in range(n):
            grads = make(d)
            if d:
                ret[d] = grads
            else:
                back[me] = grads
        far = [(d, peer, group) for d, peer in zip(far_slots, far_peers)]
        close = [(d, peer, group + 1) for d, peer in zip(near_slots, near_peers)]
        for d, peer, recv in (far[0], far[1], close[0], far[2], close[1], far[3], close[2]):
            remote(ret.at[d], back.at[me], kind, recv, peer)

    def value_back(d):
        grads = put(d, out_v)
        return jnp.where(low_half, grads[:half], swap_halves(grads[half:])).astype(bf16)

    give_back(ret_v, back_v, 4, 6, value_back)

    wait_bytes(got_v.at[1:], recv_sem.at[5])
    for d in range(n):
        placed = jnp.where(low_cap, dot(pick(d), unfold(got_v, send_v, d)), 0.0)
        region_v[:, d] = placed.astype(bf16).reshape(n, slot, width)

    my_scale = scale_ref[me] * root

    def grad_step(r, carry):
        value_low = region_v[r].reshape(capacity, width)
        g = region_g[r].reshape(capacity, width)
        qk = region_qk[r].reshape(capacity, width)
        value_t = jnp.transpose(value_low.astype(f32))[:head_size].astype(bf16)
        g_t = jnp.transpose(g.astype(f32))[:head_size]
        key_t = jnp.transpose(qk.astype(f32))[head_size:].astype(bf16)
        attended = dot(value_t, probs_low[r])
        delta = jnp.sum(g_t * attended, axis=0, keepdims=True)
        dprobs = lax.dot_general(value_low, g, CONTRACT_LANES, preferred_element_type=f32)
        dscores[r] = (probs[r] * (dprobs - delta)).astype(bf16)
        grads = dot(dscores[r], qk)
        raw_t = dot(key_t, dscores[r]).astype(bf16).astype(f32) * my_scale
        raw = jnp.transpose(jnp.concatenate([raw_t, raw_t], axis=0))
        grads = jnp.where(low_cap, grads, raw)
        out_kq[:, r] = grads.astype(bf16).reshape(n, slot, width)
        return carry

    lax.fori_loop(0, n, grad_step, 0, unroll=n)

    give_back(ret_kq, back_kq, 5, 8, lambda d: put(d, out_kq).astype(bf16))

    def unpack(half_of_tiles, unpack_pair):
        for k in range(quad // 2):
            pair = half_of_tiles * (quad // 2) + k
            unpack_pair(2 * pair, pl.ds(pl.multiple_of(pair * width, width), width))

    def unpack_v(one, cols):
        v0, v1 = back_v[one].astype(f32), back_v[one + 1].astype(f32)
        grad_v[:half, cols] = jnp.where(low_half, v0, swap_halves(v1)).astype(bf16)
        grad_v[half:, cols] = jnp.where(low_half, swap_halves(v0), v1).astype(bf16)

    def unpack_kq(one, cols):
        kq0, kq1 = back_kq[one].astype(f32), back_kq[one + 1].astype(f32)
        grad_k[:, cols] = jnp.where(low, kq0, swap_halves(kq1)).astype(bf16)
        grad_q[:, cols] = jnp.where(low, swap_halves(kq0), kq1).astype(bf16)

    wait_bytes(back_v.at[: quad - 1], recv_sem.at[7])
    wait_bytes(back_v.at[:quad], recv_sem.at[6])
    unpack(bits[2], unpack_v)
    unpack(1 - bits[2], unpack_v)
    wait_bytes(back_kq.at[: quad - 1], recv_sem.at[9])
    unpack(bits[2], unpack_kq)
    wait_bytes(back_kq.at[:quad], recv_sem.at[8])
    unpack(1 - bits[2], unpack_kq)
    for kind, refs in enumerate((got_place, send_qk, send_g, send_v, ret_v, ret_kq)):
        wait_bytes(refs.at[1:], send_sem.at[kind])


def store_kernel(q_ref, k_ref, v_ref, oq_hbm, ok_hbm, ov_hbm, sem):
    pieces = 4
    rows = q_ref.shape[0] // pieces
    pairs = ((q_ref, oq_hbm), (k_ref, ok_hbm), (v_ref, ov_hbm))
    for p in range(pieces):
        for i, (src, dst) in enumerate(pairs):
            part = slice(p * rows, (p + 1) * rows)
            pltpu.make_async_copy(src.at[part], dst.at[part], sem.at[i]).start()
    for i, (src, dst) in enumerate(pairs):
        pltpu.make_async_copy(src, dst, sem.at[i]).wait()


def by_heads(queries, key_rows, value_rows, grad_out, owner_shard, logit_scale):
    n = lax.axis_size("tile")
    tokens, columns = queries.shape
    head_size = columns // n
    capacity = 2 * tokens
    slot = capacity // n
    width = 2 * head_size
    bf16, f32 = jnp.bfloat16, jnp.float32
    vmem = pl.BlockSpec(memory_space=pltpu.VMEM)
    anywhere = pl.BlockSpec(memory_space=pltpu.HBM)
    full = pltpu.VMEM((n, tokens, width), bf16)
    folded = pltpu.VMEM((n, tokens // 2, width), bf16)
    region = pltpu.VMEM((n, n, slot, width), bf16)
    square = (n, capacity, capacity)
    grant = 67043328 - 6 * tokens * columns - 64 * 1024
    grads = pl.pallas_call(
        functools.partial(exchange_kernel, n, slot, head_size),
        out_shape=(pltpu.VMEM((tokens, columns), bf16),) * 3,
        in_specs=[anywhere] * 6,
        out_specs=(vmem, vmem, vmem),
        scratch_shapes=[pltpu.VMEM((1, tokens), jnp.int32), pltpu.SMEM((n,), f32)]
        + [pltpu.VMEM((4, tokens, columns), bf16)]
        + [pltpu.VMEM((1, tokens), f32), full, folded, folded]
        + [pltpu.VMEM((n, 1, tokens), f32), full, folded, folded]
        + [pltpu.VMEM((n, capacity, width), bf16), region, region, region, region]
        + [pltpu.VMEM((n, capacity, 128), f32), pltpu.VMEM(square, f32)]
        + [pltpu.VMEM(square, bf16), pltpu.VMEM(square, bf16)]
        + [region, region, folded, full, folded, full]
        + [pltpu.SemaphoreType.DMA((4,)), pltpu.SemaphoreType.DMA((6,))]
        + [pltpu.SemaphoreType.DMA((10,))],
        compiler_params=pltpu.CompilerParams(
            collective_id=0, has_side_effects=True, vmem_limit_bytes=grant
        ),
    )(owner_shard.reshape(1, tokens), logit_scale, queries, key_rows, value_rows, grad_out)
    out = jax.ShapeDtypeStruct((tokens, columns), bf16)
    return pl.pallas_call(
        store_kernel,
        out_shape=(out, out, out),
        in_specs=[vmem, vmem, vmem],
        out_specs=(anywhere, anywhere, anywhere),
        scratch_shapes=[pltpu.SemaphoreType.DMA((3,))],
        compiler_params=pltpu.CompilerParams(vmem_limit_bytes=1024 * 1024),
    )(*grads)


def attend_heads(query_heads, key_heads, value_heads, dout_heads, live_rows):
    pair_mask = live_rows[None, :, None] & live_rows[None, None, :]
    scores = jnp.einsum("ihe,jhe->hij", query_heads, key_heads, preferred_element_type=jnp.float32)
    scores = jnp.where(pair_mask, scores, -1e30)
    row_max = jnp.max(scores, axis=2, keepdims=True)
    raw_weights = jnp.where(pair_mask, jnp.exp(scores - row_max), 0.0)
    row_sum = jnp.sum(raw_weights, axis=2, keepdims=True)
    row_sum = jnp.where(live_rows[None, :, None], row_sum, 1.0)
    weights = raw_weights / row_sum
    weights_low = weights.astype(jnp.bfloat16)
    attended = jnp.einsum(
        "hij,jhe->ihe", weights_low, value_heads, preferred_element_type=jnp.float32
    )
    row_delta = jnp.sum(dout_heads.astype(jnp.float32) * attended, axis=2)
    dprobs = jnp.einsum("ihe,jhe->hij", dout_heads, value_heads, preferred_element_type=jnp.float32)
    dscores = (weights * (dprobs - jnp.transpose(row_delta)[:, :, None])).astype(jnp.bfloat16)
    grad_value = jnp.einsum(
        "hij,ihe->jhe", weights_low, dout_heads, preferred_element_type=jnp.float32
    ).astype(jnp.bfloat16)
    grad_key = jnp.einsum(
        "hij,ihe->jhe", dscores, query_heads, preferred_element_type=jnp.float32
    ).astype(jnp.bfloat16)
    grad_raw = jnp.einsum(
        "hij,jhe->ihe", dscores, key_heads, preferred_element_type=jnp.float32
    ).astype(jnp.bfloat16)
    return (grad_raw, grad_key, grad_value)


def attend_items(query_items, key_items, value_items, dout_items, live_rows):
    capacity = query_items.shape[0]
    item_count = query_items.shape[1]
    head_size = query_items.shape[2] // 2
    outputs = ([], [], [])
    for item_index in range(item_count):
        halves = ([], [], [])
        for half_index in range(2):
            lower = half_index * head_size
            upper = lower + head_size
            pieces = attend_heads(
                query_items[:, item_index, lower:upper].reshape(capacity, 1, head_size),
                key_items[:, item_index, lower:upper].reshape(capacity, 1, head_size),
                value_items[:, item_index, lower:upper].reshape(capacity, 1, head_size),
                dout_items[:, item_index, lower:upper].reshape(capacity, 1, head_size),
                live_rows,
            )
            for holder, piece in zip(halves, pieces):
                holder.append(piece.reshape(capacity, head_size))
        for holder, parts_list in zip(outputs, halves):
            holder.append(jnp.concatenate(parts_list, axis=1))
    return tuple((jnp.stack(holder, axis=1) for holder in outputs))


def slot_places(owner_shard, shards, slot):
    one_hot = (owner_shard[:, None] == jnp.arange(shards, dtype=jnp.int32)[None, :]).astype(
        jnp.int32
    )
    before = jnp.cumsum(one_hot, axis=0) - one_hot
    rank = jnp.sum(before * one_hot, axis=1)
    return owner_shard * slot + rank


def by_regions(queries, key_rows, value_rows, grad_out, owner_shard, logit_scale):
    shards = lax.axis_size("tile")
    tok_rows, columns = queries.shape
    heads_here = logit_scale.shape[0]
    head_size = columns // heads_here
    capacity = 2 * tok_rows
    slot = capacity // shards
    pairs = heads_here // 2
    width = 2 * head_size
    slot_index = slot_places(owner_shard, shards, slot)
    scale_cols = jnp.repeat(logit_scale / math.sqrt(head_size), head_size)
    scaled = (queries.astype(jnp.float32) * scale_cols).astype(jnp.bfloat16)

    def spread(source):
        return jnp.zeros((capacity,) + source.shape[1:], source.dtype).at[slot_index].set(source)

    sent_query = spread(scaled)
    sent_key = spread(key_rows)
    sent_value = spread(value_rows)
    sent_dout = spread(grad_out)
    flags = spread(jnp.ones((tok_rows,), jnp.int32))
    got_query, got_key, got_value, got_dout, got_flags = (
        lax.all_to_all(sent_query, "tile", split_axis=0, concat_axis=0, tiled=True),
        lax.all_to_all(sent_key, "tile", split_axis=0, concat_axis=0, tiled=True),
        lax.all_to_all(sent_value, "tile", split_axis=0, concat_axis=0, tiled=True),
        lax.all_to_all(sent_dout, "tile", split_axis=0, concat_axis=0, tiled=True),
        lax.all_to_all(flags, "tile", split_axis=0, concat_axis=0, tiled=True),
    )
    grad_raw, grad_key, grad_value = attend_items(
        got_query.reshape(capacity, pairs, width),
        got_key.reshape(capacity, pairs, width),
        got_value.reshape(capacity, pairs, width),
        got_dout.reshape(capacity, pairs, width),
        got_flags > 0,
    )
    returned = (
        lax.all_to_all(
            grad_raw.reshape(capacity, columns), "tile", split_axis=0, concat_axis=0, tiled=True
        ),
        lax.all_to_all(
            grad_key.reshape(capacity, columns), "tile", split_axis=0, concat_axis=0, tiled=True
        ),
        lax.all_to_all(
            grad_value.reshape(capacity, columns), "tile", split_axis=0, concat_axis=0, tiled=True
        ),
    )
    grad_queries = (returned[0][slot_index].astype(jnp.float32) * scale_cols).astype(jnp.bfloat16)
    return (grad_queries, returned[1][slot_index], returned[2][slot_index])


def local(queries, key_rows, value_rows, grad_out, owner_shard, logit_scale):
    shards = lax.axis_size("tile")
    tokens, columns = queries.shape
    heads_here = logit_scale.shape[0]
    slot = 2 * tokens // shards
    fits = (
        shards == heads_here == 8
        and columns == heads_here * 64
        and slot % 16 == 0
        and (2 * tokens) % 128 == 0
        and tokens % 32 == 0
    )
    plan = by_heads if fits else by_regions
    return plan(queries, key_rows, value_rows, grad_out, owner_shard, logit_scale)


def solution(mesh):
    return jax.shard_map(
        local,
        mesh=mesh,
        in_specs=(
            P(("pages", "tile"), "mp"),
            P(("pages", "tile"), "mp"),
            P(("pages", "tile"), "mp"),
            P(("pages", "tile"), "mp"),
            P(("pages", "tile")),
            P("mp"),
        ),
        out_specs=(
            P(("pages", "tile"), "mp"),
            P(("pages", "tile"), "mp"),
            P(("pages", "tile"), "mp"),
        ),
        check_vma=False,
    )
```
